512 devices in a mesh: section: 8 (over x, core), replica: 64 (over z, y).
Axes of the slice: x: 4, y: 8, z: 8, core: 2. Of those that a mesh axis runs over, the one named last changes fastest.
Arguments:
- pending_section_entries: bfloat16 [8, 128, 14, 14, 512], P('section', 'replica'), may hold values from -40 to 40
- arriving_microsets: bfloat16 [1, 128, 14, 14, 512], P(None, 'replica'), may hold values from -40 to 40
- opening_filter_kernel: bfloat16 [8, 3, 3, 512, 512], P('section'), may hold values from -0.09375 to 0.09375
- closing_filter_kernel: bfloat16 [8, 3, 3, 512, 512], P('section'), may hold values from -0.09375 to 0.09375
- stretch_factors: float32 [8, 2, 512], P('section'), may hold values from 0.5 to 1.5
- shift_terms: float32 [8, 2, 512], P('section'), may hold values from -3 to 3
Outputs:
- produced: bfloat16 [8, 2, 128, 14, 14, 512], P('section', None, 'replica')
The draws below stay inside these ranges and needn't reach their ends.
All inputs are finite; a program needn't handle non-finite values.
Results may differ from the reference program's by a relative error of at most 0.0084.
Values may be sent and summed in bfloat16 or wider, within the bound.
No kernel may reach another device: no remote copies, remote signals or barrier semaphores. Data moves between devices by JAX's collectives and lax.ppermute only.
A program may use at most 64 MiB of HBM per device.

```python
import jax
import jax.numpy as jnp
from jax import lax

C = 512
H = 14
W = 14
IMG_DEV = 2
TICKS = 2
SECTIONS = 8
IMAGES = 128


def replica_pattern(count):
    owner = jnp.arange(count) // IMG_DEV
    parity = jnp.where(owner % 2 == 1, 1.8, 1.0 / 1.8)
    triple = jnp.where(owner % 3 == 0, 1.6, 0.8)
    return (parity * triple).astype(jnp.float32)


def image_scales(key, count):
    steps = jnp.arange(count).astype(jnp.float32) / max(count - 1, 1)
    spread = 3.0 ** steps
    return spread * replica_pattern(count)


def draw_field(key, lead):
    keys = jax.random.split(key, 3)
    tensor_shape = (lead, IMAGES, H, W, C)
    base = jax.random.normal(keys[0], tensor_shape, jnp.float32)
    pixel = jnp.exp(jax.random.uniform(keys[1], (lead, IMAGES, H, W, 1), jnp.float32) * jnp.log(10.0)) / 3.0
    norm_scales = image_scales(keys[2], IMAGES).reshape(1, IMAGES, 1, 1, 1)
    return jnp.clip(base * pixel * norm_scales, -40.0, 40.0)


def draw_pending_section_entries(key, part):
    return draw_field(jax.random.fold_in(key, 11), SECTIONS).astype(jnp.bfloat16)


def draw_arriving_microsets(key, part):
    return draw_field(jax.random.fold_in(key, 23), TICKS - 1).astype(jnp.bfloat16)


def shard_levels(own_key, extent, cuts, low, largest):
    level, own = 1.0, jax.random.fold_in(own_key, 6)
    for dim, shards_of in cuts:
        draws = jnp.exp(jax.random.uniform(jax.random.fold_in(own, dim), (shards_of,), jnp.float32, low / len(cuts), largest / len(cuts)))
        level = level * jnp.repeat(draws, extent[dim] // shards_of).reshape([-1 if axis == dim else 1 for axis in range(len(extent))])
    return level


def gaussian(key, shape, deviation, bound, pieces=(), kind=jnp.bfloat16):
    entries = deviation * jax.random.normal(key, shape, jnp.float32)
    if pieces:
        entries = entries * shard_levels(key, shape, pieces, -0.22, 0.18)
    return jnp.clip(entries, -bound, bound).astype(kind)


def setup_inputs(seed: int = 0) -> dict:
    key_list = jax.random.split(jax.random.key(seed), 7)
    pending_section_entries = draw_pending_section_entries(jax.random.fold_in(key_list[6], 71), 0)
    arriving_microsets = draw_arriving_microsets(jax.random.fold_in(key_list[6], 71), 0)
    opening_filter_kernel = gaussian(key_list[2], (SECTIONS, 3, 3, C, C), (9 * C) ** -0.5, 0.09375, ((0, 8),))
    closing_filter_kernel = gaussian(key_list[3], (SECTIONS, 3, 3, C, C), (9 * C) ** -0.5, 0.09375, ((0, 8),))
    stretch_factors = jnp.clip(0.5 + 1.0 * jax.random.uniform(key_list[4], (SECTIONS, 2, C), jnp.float32) ** shard_levels(key_list[4], (SECTIONS, 2, C), ((0, 8),), -0.2, 0.2), 0.5, 1.5)
    shift_terms = gaussian(key_list[5], (SECTIONS, 2, C), 0.5, 3.0, ((0, 8),), jnp.float32)
    return dict(pending_section_entries=pending_section_entries, arriving_microsets=arriving_microsets, opening_filter_kernel=opening_filter_kernel, closing_filter_kernel=closing_filter_kernel, stretch_factors=stretch_factors, shift_terms=shift_terms)


def convolve(maps, kernel):
    return lax.conv_general_dilated(maps, kernel, (1, 1), 'SAME', dimension_numbers=('NHWC', 'HWIO', 'NHWC'), preferred_element_type=jnp.float32)

def layer(maps, kernel, gain, bias):
    conv_out = convolve(maps, kernel)
    mean = lax.optimization_barrier(jnp.mean(conv_out, axis=(0, 1, 2)))
    centred = conv_out - mean
    var = lax.optimization_barrier(jnp.mean(centred * centred, axis=(0, 1, 2)))
    scale = gain * lax.rsqrt(var + 1e-05)
    offset = bias - mean * scale
    stored = lax.optimization_barrier(conv_out.astype(jnp.bfloat16)).astype(jnp.float32)
    return jnp.maximum(stored * scale + offset, 0.0).astype(jnp.bfloat16)

def section_step(packed):
    maps, first, second, gain, bias = packed
    hidden = layer(maps, first, gain[0], bias[0])
    return layer(hidden, second, gain[1], bias[1])

def reference(pending_section_entries, arriving_microsets, opening_filter_kernel, closing_filter_kernel, stretch_factors, shift_terms):
    feed_examples = pending_section_entries
    results = []
    for tick in range(TICKS):
        outputs = lax.map(section_step, (feed_examples, opening_filter_kernel, closing_filter_kernel, stretch_factors, shift_terms))
        results.append(outputs)
        if tick + 1 < TICKS:
            feed_examples = jnp.concatenate([arriving_microsets[tick][None], outputs[:-1]], axis=0)
    return jnp.stack(results, axis=1)
```

```python
import jax
import jax.numpy as jnp
from jax import lax
from jax.sharding import PartitionSpec as P

TICKS = 2


def from_behind(shard, axis, by):
    length = lax.axis_size(axis)
    pairs = [(i, i + by) for i in range(length) if 0 <= i + by < length]
    return lax.ppermute(shard, axis, pairs)


def convolve(maps, kernel):
    return lax.conv_general_dilated(
        maps,
        kernel,
        (1, 1),
        "SAME",
        dimension_numbers=("NHWC", "HWIO", "NHWC"),
        preferred_element_type=jnp.float32,
    )


def batch_statistics(conv_out, replica_total):
    members = lax.axis_size("replica")
    count = replica_total // members
    mean = jnp.sum(conv_out, axis=(0, 1, 2)) / count
    centred = conv_out - mean
    squares = jnp.sum(centred * centred, axis=(0, 1, 2))
    packed = jnp.concatenate([mean.reshape(4, 128), squares.reshape(4, 128)], axis=0)
    copies = jnp.broadcast_to(packed, (members, 8, 128))
    gathered = lax.all_to_all(copies, "replica", 0, 0)
    means = gathered[:, :4].reshape(members, 512)
    mean = jnp.sum(means, axis=0) / members
    apart = means - mean
    spread = jnp.sum(gathered[:, 4:], axis=0).reshape(512) + count * jnp.sum(apart * apart, axis=0)
    return (mean, spread / replica_total)


def coefficients(conv_out, gain, bias, replica_total):
    mean, var = batch_statistics(conv_out, replica_total)
    scale = gain * lax.rsqrt(var + 1e-05)
    return (scale, bias - mean * scale)


def store(conv_out):
    return lax.optimization_barrier(conv_out.astype(jnp.bfloat16))


def normalize(stored, scale, offset):
    return jnp.maximum(stored.astype(jnp.float32) * scale + offset, 0.0).astype(jnp.bfloat16)


def body(
    pending_section_entries,
    arriving_microsets,
    opening_filter_kernel,
    closing_filter_kernel,
    stretch_factors,
    shift_terms,
):
    replica_total = (
        lax.axis_size("replica")
        * pending_section_entries.shape[1]
        * pending_section_entries.shape[2]
        * pending_section_entries.shape[3]
    )
    is_first = lax.axis_index("section") == 0
    first_kernel = opening_filter_kernel[0]
    second_kernel = closing_filter_kernel[0]
    current_feature_map = pending_section_entries[0]
    results = []
    for tick in range(TICKS):
        conv_one = convolve(current_feature_map, first_kernel)
        scale_one, offset_one = coefficients(
            conv_one, stretch_factors[0, 0], shift_terms[0, 0], replica_total
        )
        hidden = normalize(store(conv_one), scale_one, offset_one)
        conv_two = convolve(hidden, second_kernel)
        stored_two = store(conv_two)
        last = tick + 1 == TICKS
        scale_two, offset_two = coefficients(
            conv_two, stretch_factors[0, 1], shift_terms[0, 1], replica_total
        )
        output = normalize(stored_two, scale_two, offset_two)
        if not last:
            moved = from_behind(output, "section", 1)
        results.append(output)
        if not last:
            current_feature_map = jnp.where(is_first, arriving_microsets[tick], moved)
    return jnp.stack(results, axis=0)[None]


def solution(mesh):
    in_specs = (
        P("section", "replica", None, None, None),
        P(None, "replica", None, None, None),
        P("section", None, None, None, None),
        P("section", None, None, None, None),
        P("section", None, None),
        P("section", None, None),
    )
    out_specs = P("section", None, "replica", None, None, None)
    return jax.shard_map(body, mesh=mesh, in_specs=in_specs, out_specs=out_specs, check_vma=False)
```

```python
import jax
import jax.numpy as jnp
from jax import lax
from jax.experimental import pallas as pl
from jax.experimental.pallas import tpu as pltpu
from jax.sharding import PartitionSpec as P

TICKS = 2
LANES = 128
EPS = 1e-05


class Plan:
    def __init__(self, images, height, width, channels, members):
        self.images, self.height, self.width, self.channels = images, height, width, channels
        self.members = members
        self.wide = 16
        self.line = self.wide * images
        self.rows = height * self.line
        self.groups = channels // LANES
        self.count = images * height * width

    def real_rows(self):
        row = lax.broadcasted_iota(jnp.int32, (self.rows, LANES), 0)
        return row % self.line < self.width * self.images


def fill_shifted(plan, padded):
    line, rows, step = plan.line, plan.rows, plan.images
    padded[0, pl.ds(line, rows), :] = padded[1, pl.ds(line - step, rows), :]
    padded[2, pl.ds(line, rows), :] = padded[1, pl.ds(line + step, rows), :]


def zero_borders(plan, padded):
    border = jnp.zeros((plan.line, plan.channels), jnp.bfloat16)
    for shift in range(3):
        padded[shift, pl.ds(0, plan.line), :] = border
        padded[shift, pl.ds(plan.line + plan.rows, plan.line), :] = border


def convolve_and_measure(plan, padded, tap, stored_ref, packed_ref):
    pieces, filters = [], []
    for kh in range(3):
        for kw in range(3):
            pieces.append(padded[kw, pl.ds(kh * plan.line, plan.rows), :])
            filters.append(tap(kh, kw))
    conv_out = jnp.dot(
        jnp.concatenate(pieces, axis=1),
        jnp.concatenate(filters, axis=0),
        preferred_element_type=jnp.float32,
    )
    stored_ref[...] = conv_out.astype(jnp.bfloat16)
    real = plan.real_rows()
    means, squares = [], []
    for group in range(plan.groups):
        values = jnp.where(real, conv_out[:, group * LANES : (group + 1) * LANES], 0.0)
        mean = jnp.sum(values, axis=0, keepdims=True) / plan.count
        centred = jnp.where(real, values - mean, 0.0)
        means.append(mean)
        squares.append(jnp.sum(centred * centred, axis=0, keepdims=True))
    packed = jnp.concatenate(means + squares, axis=0)
    packed_ref[...] = jnp.broadcast_to(packed[None], packed_ref.shape)


def join(plan, gathered, gain, bias):
    groups = plan.groups
    means = gathered[:, :groups, :]
    mean = jnp.sum(means, axis=0) / plan.members
    apart = means - mean[None]
    spread = jnp.sum(gathered[:, groups:, :], axis=0) + plan.count * jnp.sum(apart * apart, axis=0)
    scale = gain * lax.rsqrt(spread / (plan.count * plan.members) + EPS)
    return scale, bias - mean * scale


def normalize_into(plan, stored_ref, scale, offset, write):
    real = plan.real_rows()
    for group in range(plan.groups):
        lanes = slice(group * LANES, (group + 1) * LANES)
        values = stored_ref[:, lanes].astype(jnp.float32) * scale[group : group + 1] + offset[group : group + 1]
        write(lanes, jnp.where(real, jnp.maximum(values, 0.0), 0.0).astype(jnp.bfloat16))


def start_filters(kernel_hbm, kernel_vmem, sems):
    copies = {}
    for kh in range(3):
        for kw in range(3):
            copy = pltpu.make_async_copy(kernel_hbm.at[kh, kw], kernel_vmem.at[kh, kw], sems.at[kh, kw])
            copy.start()
            copies[kh, kw] = copy

    def tap(kh, kw):
        copies[kh, kw].wait()
        return kernel_vmem[kh, kw]

    return tap


def conv_layer(plan, body, operands, kernel):
    whole = pl.BlockSpec(memory_space=pltpu.VMEM)

    def run(*refs):
        ins = refs[: len(operands)]
        kernel_hbm, stored_ref, packed_ref, padded, kernel_vmem, sems = refs[len(operands) :]
        tap = start_filters(kernel_hbm, kernel_vmem, sems)
        zero_borders(plan, padded)
        body(padded, *ins)
        fill_shifted(plan, padded)
        convolve_and_measure(plan, padded, tap, stored_ref, packed_ref)

    channels = plan.channels
    return pl.pallas_call(
        run,
        in_specs=[whole] * len(operands) + [pl.BlockSpec(memory_space=pltpu.HBM)],
        out_specs=[whole, whole],
        out_shape=[
            jax.ShapeDtypeStruct((plan.rows, channels), jnp.bfloat16),
            jax.ShapeDtypeStruct((plan.members, 2 * plan.groups, LANES), jnp.float32),
        ],
        scratch_shapes=[
            pltpu.VMEM((3, plan.rows + 2 * plan.line, channels), jnp.bfloat16),
            pltpu.VMEM((3, 3, channels, channels), jnp.bfloat16),
            pltpu.SemaphoreType.DMA((3, 3)),
        ],
        compiler_params=pltpu.CompilerParams(vmem_limit_bytes=32 << 20),
    )(*operands, kernel)


def inner(plan):
    return pl.ds(plan.line, plan.rows)


def layer_of_map(plan, rows, kernel):
    def body(padded, rows_ref):
        padded[1, inner(plan), :] = rows_ref[...]

    return conv_layer(plan, body, [rows], kernel)


def layer_of_stored(plan, stored, gathered, gain, bias, kernel):
    def body(padded, stored_ref, gathered_ref, gain_ref, bias_ref):
        scale, offset = join(plan, gathered_ref[...], gain_ref[...], bias_ref[...])

        def write(lanes, values):
            padded[1, inner(plan), lanes] = values

        normalize_into(plan, stored_ref, scale, offset, write)

    return conv_layer(plan, body, [stored, gathered, gain, bias], kernel)


def layer_of_moved(plan, stored, coefficients, rows, is_first, kernel):
    def body(padded, stored_ref, coefficients_ref, rows_ref, first_ref):
        first = jnp.broadcast_to(first_ref[...], (plan.rows, LANES)) > 0.5

        def write(lanes, values):
            padded[1, inner(plan), lanes] = jnp.where(first, rows_ref[:, lanes], values)

        both = coefficients_ref[...]
        normalize_into(plan, stored_ref, both[: plan.groups], both[plan.groups :], write)

    return conv_layer(plan, body, [stored, coefficients, rows, is_first], kernel)


def finish(plan, stored, scale, offset):
    whole = pl.BlockSpec(memory_space=pltpu.VMEM)

    def run(stored_ref, scale_ref, offset_ref, out_ref):
        def write(lanes, values):
            out_ref[:, lanes] = values

        normalize_into(plan, stored_ref, scale_ref[...], offset_ref[...], write)

    return pl.pallas_call(
        run,
        in_specs=[whole] * 3,
        out_specs=whole,
        out_shape=jax.ShapeDtypeStruct(stored.shape, stored.dtype),
    )(stored, scale, offset)


def to_rows(plan, maps):
    rows = jnp.transpose(maps, (1, 2, 0, 3))
    rows = jnp.pad(rows, ((0, 0), (0, plan.wide - plan.width), (0, 0), (0, 0)))
    return rows.reshape(plan.rows, plan.channels)


def to_maps(plan, rows):
    maps = rows.reshape(plan.height, plan.wide, plan.images, plan.channels)[:, : plan.width]
    return jnp.transpose(maps, (2, 0, 1, 3))


def from_behind(value, axis):
    pairs = [(i, i + 1) for i in range(lax.axis_size(axis) - 1)]
    return lax.ppermute(value, axis, pairs)


def exchange(copies):
    return lax.all_to_all(copies, "replica", 0, 0)


def body(
    pending_section_entries,
    arriving_microsets,
    opening_filter_kernel,
    closing_filter_kernel,
    stretch_factors,
    shift_terms,
):
    _, images, height, width, channels = pending_section_entries.shape
    plan = Plan(images, height, width, channels, lax.axis_size("replica"))
    first_kernel = opening_filter_kernel[0]
    second_kernel = closing_filter_kernel[0]
    gain = stretch_factors[0].reshape(2, plan.groups, LANES)
    bias = shift_terms[0].reshape(2, plan.groups, LANES)
    is_first = jnp.broadcast_to((lax.axis_index("section") == 0).astype(jnp.float32), (1, LANES))
    stored, packed = layer_of_map(plan, to_rows(plan, pending_section_entries[0]), first_kernel)
    results = []
    for tick in range(TICKS):
        stored, packed = layer_of_stored(plan, stored, exchange(packed), gain[0], bias[0], second_kernel)
        last = tick + 1 == TICKS
        if not last:
            moved = from_behind(stored, "section")
        scale, offset = join(plan, exchange(packed), gain[1], bias[1])
        if not last:
            coefficients = from_behind(jnp.concatenate([scale, offset], axis=0), "section")
        results.append(to_maps(plan, finish(plan, stored, scale, offset)))
        if not last:
            rows = to_rows(plan, arriving_microsets[tick])
            stored, packed = layer_of_moved(plan, moved, coefficients, rows, is_first, first_kernel)
    return jnp.stack(results, axis=0)[None]


def solution(mesh):
    in_specs = (
        P("section", "replica", None, None, None),
        P(None, "replica", None, None, None),
        P("section", None, None, None, None),
        P("section", None, None, None, None),
        P("section", None, None),
        P("section", None, None),
    )
    out_specs = P("section", None, "replica", None, None, None)
    return jax.shard_map(body, mesh=mesh, in_specs=in_specs, out_specs=out_specs, check_vma=False)
```

```python
import jax
import jax.numpy as jnp
from jax import lax
from jax.experimental import pallas as pl
from jax.experimental.pallas import tpu as pltpu
from jax.sharding import PartitionSpec as P

TICKS = 2
LANES = 128
EPS = 1e-05


class Plan:
    def __init__(self, images, height, width, channels, members):
        self.images, self.height, self.width, self.channels = images, height, width, channels
        self.members = members
        self.wide = 16
        self.line = self.wide * images
        self.rows = height * self.line
        self.groups = channels // LANES
        self.count = images * height * width

    def real_rows(self):
        row = lax.broadcasted_iota(jnp.int32, (self.rows, LANES), 0)
        return row % self.line < self.width * self.images


def fill_shifted(plan, padded):
    line, rows, step = plan.line, plan.rows, plan.images
    padded[0, pl.ds(line, rows), :] = padded[1, pl.ds(line - step, rows), :]
    padded[2, pl.ds(line, rows), :] = padded[1, pl.ds(line + step, rows), :]


def zero_borders(plan, padded):
    border = jnp.zeros((plan.line, plan.channels), jnp.bfloat16)
    for shift in range(3):
        padded[shift, pl.ds(0, plan.line), :] = border
        padded[shift, pl.ds(plan.line + plan.rows, plan.line), :] = border


def convolve_and_measure(plan, padded, tap, lines, stored_ref, packed_ref):
    conv_out = None
    for start in range(0, 3, lines):
        pieces, filters = [], []
        for kh in range(start, start + lines):
            for kw in range(3):
                pieces.append(padded[kw, pl.ds(kh * plan.line, plan.rows), :])
                filters.append(tap(kh, kw))
        part = jnp.dot(
            jnp.concatenate(pieces, axis=1),
            jnp.concatenate(filters, axis=0),
            preferred_element_type=jnp.float32,
        )
        conv_out = part if conv_out is None else conv_out + part
    stored_ref[...] = conv_out.astype(jnp.bfloat16)
    real = plan.real_rows()
    means, squares = [], []
    for group in range(plan.groups):
        values = jnp.where(real, conv_out[:, group * LANES : (group + 1) * LANES], 0.0)
        mean = jnp.sum(values, axis=0, keepdims=True) / plan.count
        centred = jnp.where(real, values - mean, 0.0)
        means.append(mean)
        squares.append(jnp.sum(centred * centred, axis=0, keepdims=True))
    packed = jnp.concatenate(means + squares, axis=0)
    packed_ref[...] = jnp.broadcast_to(packed[None], packed_ref.shape)


def join(plan, gathered, gain, bias):
    groups = plan.groups
    means = gathered[:, :groups, :]
    mean = jnp.sum(means, axis=0) / plan.members
    apart = means - mean[None]
    spread = jnp.sum(gathered[:, groups:, :], axis=0) + plan.count * jnp.sum(apart * apart, axis=0)
    scale = gain * lax.rsqrt(spread / (plan.count * plan.members) + EPS)
    return scale, bias - mean * scale


def normalize_into(plan, stored_ref, scale, offset, write):
    real = plan.real_rows()
    for group in range(plan.groups):
        lanes = slice(group * LANES, (group + 1) * LANES)
        values = stored_ref[:, lanes].astype(jnp.float32) * scale[group : group + 1] + offset[group : group + 1]
        write(lanes, jnp.where(real, jnp.maximum(values, 0.0), 0.0).astype(jnp.bfloat16))


def in_vmem(value):
    return pltpu.with_memory_space_constraint(value, pltpu.VMEM)


def in_hbm(value):
    return pltpu.with_memory_space_constraint(value, pltpu.HBM)


def start_filters(kernel_hbm, kernel_vmem, sems):
    copies = {}
    for kh in range(3):
        for kw in range(3):
            copy = pltpu.make_async_copy(kernel_hbm.at[kh, kw], kernel_vmem.at[kh, kw], sems.at[kh, kw])
            copy.start()
            copies[kh, kw] = copy

    def tap(kh, kw):
        copies[kh, kw].wait()
        return kernel_vmem[kh, kw]

    return tap


def filter_scratch(kernel):
    return [pltpu.VMEM(kernel.shape, kernel.dtype), pltpu.SemaphoreType.DMA((3, 3))]


def layer_outputs(plan):
    return [
        pltpu.VMEM((plan.rows, plan.channels), jnp.bfloat16),
        pltpu.VMEM((plan.members, 2 * plan.groups, LANES), jnp.float32),
    ]


def padded_scratch(plan):
    return pltpu.VMEM((3, plan.rows + 2 * plan.line, plan.channels), jnp.bfloat16)


WHOLE = pl.BlockSpec(memory_space=pltpu.VMEM)
OUTSIDE = pl.BlockSpec(memory_space=pltpu.HBM)
PARAMS = pltpu.CompilerParams(vmem_limit_bytes=32 << 20)


def conv_layer(plan, body, operands, kernel):
    def run(*refs):
        ins = refs[: len(operands)]
        kernel_hbm, stored_ref, packed_ref, padded, kernel_vmem, sems = refs[len(operands) :]
        tap = start_filters(kernel_hbm, kernel_vmem, sems)
        zero_borders(plan, padded)
        body(padded, *ins)
        fill_shifted(plan, padded)
        convolve_and_measure(plan, padded, tap, 3, stored_ref, packed_ref)

    return pl.pallas_call(
        run,
        in_specs=[WHOLE] * len(operands) + [OUTSIDE],
        out_specs=[WHOLE, WHOLE],
        out_shape=layer_outputs(plan),
        scratch_shapes=[padded_scratch(plan)] + filter_scratch(kernel),
        compiler_params=PARAMS,
    )(*operands, in_hbm(kernel))


def inner(plan):
    return pl.ds(plan.line, plan.rows)


def spread_lines(plan, maps_ref, write):
    real = plan.width * plan.images
    blank = jnp.zeros((plan.line - real, plan.channels), jnp.bfloat16)
    for row in range(plan.height):
        write(row * plan.line, maps_ref[row].reshape(real, plan.channels))
        write(row * plan.line + real, blank)


def opening_layer(plan, maps, kernel):
    def run(maps_hbm, kernel_hbm, stored_ref, packed_ref, maps_vmem, map_sem, padded, kernel_vmem, sems):
        fetch = pltpu.make_async_copy(maps_hbm, maps_vmem, map_sem)
        fetch.start()
        tap = start_filters(kernel_hbm, kernel_vmem, sems)
        zero_borders(plan, padded)
        fetch.wait()

        def write(start, rows):
            padded[1, pl.ds(plan.line + start, rows.shape[0]), :] = rows

        spread_lines(plan, maps_vmem, write)
        fill_shifted(plan, padded)
        convolve_and_measure(plan, padded, tap, 1, stored_ref, packed_ref)

    return pl.pallas_call(
        run,
        in_specs=[OUTSIDE, OUTSIDE],
        out_specs=[WHOLE, WHOLE],
        out_shape=layer_outputs(plan),
        scratch_shapes=[
            pltpu.VMEM(maps.shape, maps.dtype),
            pltpu.SemaphoreType.DMA(()),
            padded_scratch(plan),
        ]
        + filter_scratch(kernel),
        compiler_params=PARAMS,
    )(in_hbm(maps), in_hbm(kernel))


def prepare(plan, maps):
    def run(maps_ref, rows_ref):
        def write(start, rows):
            rows_ref[pl.ds(start, rows.shape[0]), :] = rows

        spread_lines(plan, maps_ref, write)

    return pl.pallas_call(
        run,
        in_specs=[WHOLE],
        out_specs=WHOLE,
        out_shape=pltpu.VMEM((plan.rows, plan.channels), jnp.bfloat16),
        compiler_params=PARAMS,
    )(maps)


def layer_of_stored(plan, stored, gathered, gain, bias, kernel):
    def body(padded, stored_ref, gathered_ref, gain_ref, bias_ref):
        scale, offset = join(plan, gathered_ref[...], gain_ref[...], bias_ref[...])

        def write(lanes, values):
            padded[1, inner(plan), lanes] = values

        normalize_into(plan, stored_ref, scale, offset, write)

    return conv_layer(plan, body, [in_vmem(stored), gathered, gain, bias], kernel)


def layer_of_moved(plan, stored, coefficients, rows, is_first, kernel):
    def body(padded, stored_ref, coefficients_ref, rows_ref, first_ref):
        first = jnp.broadcast_to(first_ref[...], (plan.rows, LANES)) > 0.5

        def write(lanes, values):
            padded[1, inner(plan), lanes] = jnp.where(first, rows_ref[:, lanes], values)

        both = coefficients_ref[...]
        normalize_into(plan, stored_ref, both[: plan.groups], both[plan.groups :], write)

    return conv_layer(plan, body, [stored, coefficients, in_vmem(rows), is_first], kernel)


def finish(plan, stored, joined, result, tick):
    shape = (TICKS, plan.height, plan.width, plan.images, plan.channels)

    def run(stored_ref, *refs):
        out_ref = refs[-1]
        terms = [ref[...] for ref in refs[: len(joined)]]
        if len(terms) == 1:
            scale, offset = terms[0][: plan.groups], terms[0][plan.groups :]
        else:
            scale, offset = join(plan, *terms)

        def write(lanes, values):
            for row in range(plan.height):
                line = values[row * plan.line : row * plan.line + plan.width * plan.images]
                out_ref[0, row, :, :, lanes] = line.reshape(plan.width, plan.images, LANES)

        normalize_into(plan, stored_ref, scale, offset, write)

    before = [] if result is None else [result]
    return pl.pallas_call(
        run,
        grid=(1,),
        in_specs=[WHOLE] * (1 + len(joined)) + [OUTSIDE] * len(before),
        out_specs=pl.BlockSpec((1,) + shape[1:], lambda i: (tick, 0, 0, 0, 0)),
        out_shape=pltpu.HBM(shape, jnp.bfloat16),
        input_output_aliases={1 + len(joined): 0} if before else {},
        compiler_params=PARAMS,
    )(in_vmem(stored), *joined, *before)


def from_behind(value, axis):
    pairs = [(i, i + 1) for i in range(lax.axis_size(axis) - 1)]
    return lax.ppermute(value, axis, pairs)


def exchange(copies):
    return lax.all_to_all(copies, "replica", 0, 0)


def body(
    pending_section_entries,
    arriving_microsets,
    opening_filter_kernel,
    closing_filter_kernel,
    stretch_factors,
    shift_terms,
):
    _, images, height, width, channels = pending_section_entries.shape
    plan = Plan(images, height, width, channels, lax.axis_size("replica"))
    first_kernel = opening_filter_kernel[0]
    second_kernel = closing_filter_kernel[0]
    gain = stretch_factors[0].reshape(2, plan.groups, LANES)
    bias = shift_terms[0].reshape(2, plan.groups, LANES)
    is_first = jnp.broadcast_to((lax.axis_index("section") == 0).astype(jnp.float32), (1, LANES))
    order = (1, 2, 0, 3)
    stored, packed = opening_layer(
        plan, jnp.transpose(pending_section_entries[0], order), first_kernel
    )
    result = None
    for tick in range(TICKS):
        last = tick + 1 == TICKS
        if not last:
            packed, arriving = lax.optimization_barrier((packed, arriving_microsets[tick]))
            rows = prepare(plan, jnp.transpose(arriving, order))
        gathered = exchange(packed)
        if not last:
            gathered, rows = lax.optimization_barrier((gathered, rows))
        stored, packed = layer_of_stored(plan, stored, gathered, gain[0], bias[0], second_kernel)
        if last:
            result = finish(plan, stored, [exchange(packed), gain[1], bias[1]], result, tick)
        else:
            moved = from_behind(stored, "section")
            coefficients = jnp.concatenate(join(plan, exchange(packed), gain[1], bias[1]), axis=0)
            result = finish(plan, stored, [coefficients], result, tick)
            coefficients = from_behind(coefficients, "section")
            stored, packed = layer_of_moved(plan, moved, coefficients, rows, is_first, first_kernel)
    return jnp.transpose(result, (0, 3, 1, 2, 4))[None]


def solution(mesh):
    in_specs = (
        P("section", "replica", None, None, None),
        P(None, "replica", None, None, None),
        P("section", None, None, None, None),
        P("section", None, None, None, None),
        P("section", None, None),
        P("section", None, None),
    )
    out_specs = P("section", None, "replica", None, None, None)
    return jax.shard_map(body, mesh=mesh, in_specs=in_specs, out_specs=out_specs, check_vma=False)
```

```python
import jax
import jax.numpy as jnp
from jax import lax
from jax.experimental import pallas as pl
from jax.experimental.pallas import tpu as pltpu
from jax.sharding import PartitionSpec as P

TICKS = 2
LANES = 128
EPS = 1e-05


class Plan:
    def __init__(self, images, height, width, channels, members):
        self.images, self.height, self.width, self.channels = images, height, width, channels
        self.members = members
        self.wide = 16
        self.line = self.wide * images
        self.rows = height * self.line
        self.groups = channels // LANES
        self.count = images * height * width

    def real_rows(self):
        row = lax.broadcasted_iota(jnp.int32, (self.rows, LANES), 0)
        return row % self.line < self.width * self.images


def fill_shifted(plan, padded):
    line, rows, step = plan.line, plan.rows, plan.images
    padded[0, pl.ds(line, rows), :] = padded[1, pl.ds(line - step, rows), :]
    padded[2, pl.ds(line, rows), :] = padded[1, pl.ds(line + step, rows), :]


def zero_borders(plan, padded):
    border = jnp.zeros((plan.line, plan.channels), jnp.bfloat16)
    for shift in range(3):
        padded[shift, pl.ds(0, plan.line), :] = border
        padded[shift, pl.ds(plan.line + plan.rows, plan.line), :] = border


def convolve_and_measure(plan, padded, tap, stored_ref, packed_ref):
    conv_out = None
    for kh in range(3):
        for kw in range(3):
            shifted = padded[kw, pl.ds(kh * plan.line, plan.rows), :]
            part = jnp.dot(shifted, tap(kh, kw), preferred_element_type=jnp.float32)
            conv_out = part if conv_out is None else conv_out + part
    stored_ref[...] = conv_out.astype(jnp.bfloat16)
    real = plan.real_rows()
    means, deviations = [], []
    for group in range(plan.groups):
        values = jnp.where(real, conv_out[:, group * LANES : (group + 1) * LANES], 0.0)
        mean = jnp.sum(values, axis=0, keepdims=True) / plan.count
        centred = jnp.where(real, values - mean, 0.0)
        means.append(mean)
        deviations.append(jnp.sqrt(jnp.sum(centred * centred, axis=0, keepdims=True) / plan.count))
    packed_ref[...] = jnp.concatenate(means + deviations, axis=0)


def join(plan, packed, gain, bias):
    groups = plan.groups
    copies = jnp.broadcast_to(packed.astype(jnp.float16), (plan.members,) + packed.shape)
    gathered = lax.all_to_all(copies, "replica", 0, 0)
    gathered, gain, bias = lax.optimization_barrier((gathered, gain, bias))
    gathered = gathered.astype(jnp.float32)
    gain, bias = gain.reshape(groups, LANES), bias.reshape(groups, LANES)
    means, deviations = gathered[:, :groups], gathered[:, groups:]
    mean = jnp.sum(means, axis=0) / plan.members
    apart = means - mean
    var = jnp.sum(deviations * deviations + apart * apart, axis=0) / plan.members
    scale = gain * lax.rsqrt(var + EPS)
    return jnp.concatenate([scale, bias - mean * scale], axis=0)


def normalize_into(plan, stored_ref, terms, write):
    real = plan.real_rows()
    scale, offset = terms[: plan.groups], terms[plan.groups :]
    for group in range(plan.groups):
        lanes = slice(group * LANES, (group + 1) * LANES)
        values = stored_ref[:, lanes].astype(jnp.float32) * scale[group : group + 1] + offset[group : group + 1]
        write(lanes, jnp.where(real, jnp.maximum(values, 0.0), 0.0).astype(jnp.bfloat16))


def in_vmem(value):
    return pltpu.with_memory_space_constraint(value, pltpu.VMEM)


def in_hbm(value):
    return pltpu.with_memory_space_constraint(value, pltpu.HBM)


def start_filters(kernel_hbm, kernel_vmem, sems):
    copies = {}
    for kh in range(3):
        for kw in range(3):
            copy = pltpu.make_async_copy(kernel_hbm.at[kh, kw], kernel_vmem.at[kh, kw], sems.at[kh, kw])
            copy.start()
            copies[kh, kw] = copy

    def tap(kh, kw):
        copies[kh, kw].wait()
        return kernel_vmem[kh, kw]

    return tap


def filter_scratch(kernel):
    return [pltpu.VMEM(kernel.shape, kernel.dtype), pltpu.SemaphoreType.DMA((3, 3))]


def layer_outputs(plan):
    return [
        pltpu.VMEM((plan.rows, plan.channels), jnp.bfloat16),
        pltpu.VMEM((2 * plan.groups, LANES), jnp.float32),
    ]


def padded_scratch(plan):
    return pltpu.VMEM((3, plan.rows + 2 * plan.line, plan.channels), jnp.bfloat16)


WHOLE = pl.BlockSpec(memory_space=pltpu.VMEM)
OUTSIDE = pl.BlockSpec(memory_space=pltpu.HBM)
PARAMS = pltpu.CompilerParams(vmem_limit_bytes=32 << 20)


def conv_layer(plan, body, operands, kernel):
    def run(*refs):
        ins = refs[: len(operands)]
        kernel_hbm, stored_ref, packed_ref, padded, kernel_vmem, sems = refs[len(operands) :]
        tap = start_filters(kernel_hbm, kernel_vmem, sems)
        zero_borders(plan, padded)
        body(padded, *ins)
        fill_shifted(plan, padded)
        convolve_and_measure(plan, padded, tap, stored_ref, packed_ref)

    return pl.pallas_call(
        run,
        in_specs=[WHOLE] * len(operands) + [OUTSIDE],
        out_specs=[WHOLE, WHOLE],
        out_shape=layer_outputs(plan),
        scratch_shapes=[padded_scratch(plan)] + filter_scratch(kernel),
        compiler_params=PARAMS,
    )(*operands, in_hbm(kernel))


def inner(plan):
    return pl.ds(plan.line, plan.rows)


def spread_lines(plan, maps_ref, write):
    real = plan.width * plan.images
    blank = jnp.zeros((plan.line - real, plan.channels), jnp.bfloat16)
    for row in range(plan.height):
        write(row * plan.line, maps_ref[row].reshape(real, plan.channels))
        write(row * plan.line + real, blank)


def opening_layer(plan, maps, kernel):
    def run(maps_hbm, kernel_hbm, stored_ref, packed_ref, maps_vmem, map_sem, padded, kernel_vmem, sems):
        fetch = pltpu.make_async_copy(maps_hbm, maps_vmem, map_sem)
        fetch.start()
        tap = start_filters(kernel_hbm, kernel_vmem, sems)
        zero_borders(plan, padded)
        fetch.wait()

        def write(start, rows):
            padded[1, pl.ds(plan.line + start, rows.shape[0]), :] = rows

        spread_lines(plan, maps_vmem, write)
        fill_shifted(plan, padded)
        convolve_and_measure(plan, padded, tap, stored_ref, packed_ref)

    return pl.pallas_call(
        run,
        in_specs=[OUTSIDE, OUTSIDE],
        out_specs=[WHOLE, WHOLE],
        out_shape=layer_outputs(plan),
        scratch_shapes=[
            pltpu.VMEM(maps.shape, maps.dtype),
            pltpu.SemaphoreType.DMA(()),
            padded_scratch(plan),
        ]
        + filter_scratch(kernel),
        compiler_params=PARAMS,
    )(in_hbm(maps), in_hbm(kernel))


def layer_of_stored(plan, stored, terms, kernel):
    def body(padded, stored_ref, terms_ref):
        def write(lanes, values):
            padded[1, inner(plan), lanes] = values

        normalize_into(plan, stored_ref, terms_ref[...], write)

    return conv_layer(plan, body, [in_vmem(stored), terms], kernel)


def layer_of_moved(plan, stored, terms, maps, is_first, kernel):
    def body(padded, stored_ref, terms_ref, maps_ref, first_ref):
        first = jnp.broadcast_to(first_ref[...], (plan.rows, LANES)) > 0.5

        def write(lanes, values):
            arrived = padded[1, inner(plan), lanes]
            padded[1, inner(plan), lanes] = jnp.where(first, arrived, values)

        def write_line(start, rows):
            padded[1, pl.ds(plan.line + start, rows.shape[0]), :] = rows

        spread_lines(plan, maps_ref, write_line)
        normalize_into(plan, stored_ref, terms_ref[...], write)

    return conv_layer(plan, body, [in_vmem(stored), terms, in_vmem(maps), is_first], kernel)


def finish(plan, stored, terms):
    shape = (TICKS, plan.height, plan.width, plan.images, plan.channels)

    def run(*refs):
        out_ref = refs[-1]
        for tick in range(TICKS):

            def write(lanes, values, tick=tick):
                for row in range(plan.height):
                    line = values[row * plan.line : row * plan.line + plan.width * plan.images]
                    out_ref[tick, row, :, :, lanes] = line.reshape(plan.width, plan.images, LANES)

            normalize_into(plan, refs[tick], refs[TICKS + tick][...], write)

    return pl.pallas_call(
        run,
        in_specs=[WHOLE] * (2 * TICKS),
        out_specs=WHOLE,
        out_shape=pltpu.HBM(shape, jnp.bfloat16),
        compiler_params=PARAMS,
    )(*(in_vmem(value) for value in stored), *terms)


def from_behind(value, axis):
    pairs = [(i, i + 1) for i in range(lax.axis_size(axis) - 1)]
    return lax.ppermute(value, axis, pairs)


def body(
    pending_section_entries,
    arriving_microsets,
    opening_filter_kernel,
    closing_filter_kernel,
    stretch_factors,
    shift_terms,
):
    _, images, height, width, channels = pending_section_entries.shape
    plan = Plan(images, height, width, channels, lax.axis_size("replica"))
    first_kernel = opening_filter_kernel[0]
    second_kernel = closing_filter_kernel[0]
    gain = stretch_factors[0]
    bias = shift_terms[0]
    is_first = jnp.broadcast_to((lax.axis_index("section") == 0).astype(jnp.float32), (1, LANES))
    order = (1, 2, 0, 3)
    stored, packed = opening_layer(
        plan, jnp.transpose(pending_section_entries[0], order), first_kernel
    )
    kept, kept_terms = [], []
    for tick in range(TICKS):
        terms = join(plan, packed, gain[0], bias[0])
        stored, packed = layer_of_stored(plan, stored, terms, second_kernel)
        last = tick + 1 == TICKS
        if not last:
            moved = from_behind(stored, "section")
        terms = join(plan, packed, gain[1], bias[1])
        kept.append(stored)
        kept_terms.append(terms)
        if not last:
            terms = from_behind(terms, "section")
            arriving = jnp.transpose(arriving_microsets[tick], order)
            stored, packed = layer_of_moved(plan, moved, terms, arriving, is_first, first_kernel)
    result = finish(plan, kept, kept_terms)
    return jnp.transpose(result, (0, 3, 1, 2, 4))[None]


def solution(mesh):
    in_specs = (
        P("section", "replica", None, None, None),
        P(None, "replica", None, None, None),
        P("section", None, None, None, None),
        P("section", None, None, None, None),
        P("section", None, None),
        P("section", None, None),
    )
    out_specs = P("section", None, "replica", None, None, None)
    return jax.shard_map(body, mesh=mesh, in_specs=in_specs, out_specs=out_specs, check_vma=False)
```

```python
import jax
import jax.numpy as jnp
from jax import lax
from jax.experimental import pallas as pl
from jax.experimental.pallas import tpu as pltpu
from jax.sharding import PartitionSpec as P

TICKS = 2
LANES = 128
EPS = 1e-05


class Plan:
    def __init__(self, images, height, width, channels, members):
        self.images, self.height, self.width, self.channels = images, height, width, channels
        self.members = members
        self.wide = 16
        self.line = self.wide * images
        self.rows = height * self.line
        self.groups = channels // LANES
        self.count = images * height * width

    def real_rows(self):
        row = lax.broadcasted_iota(jnp.int32, (self.rows, LANES), 0)
        return row % self.line < self.width * self.images


def fill_shifted(plan, padded):
    line, rows, step = plan.line, plan.rows, plan.images
    padded[0, pl.ds(line, rows), :] = padded[1, pl.ds(line - step, rows), :]
    padded[2, pl.ds(line, rows), :] = padded[1, pl.ds(line + step, rows), :]


def zero_borders(plan, padded):
    border = jnp.zeros((plan.line, plan.channels), jnp.bfloat16)
    for shift in range(3):
        padded[shift, pl.ds(0, plan.line), :] = border
        padded[shift, pl.ds(plan.line + plan.rows, plan.line), :] = border


MIDDLE = [(0, 1), (1, 1), (2, 1)]
SIDES = [(0, 0), (1, 0), (2, 0), (0, 2), (1, 2), (2, 2)]


def convolve_and_measure(plan, padded, tap, stored_ref, packed_ref):
    conv_out = None
    for kh, kw in MIDDLE + SIDES:
        shifted = padded[kw, pl.ds(kh * plan.line, plan.rows), :]
        part = jnp.dot(shifted, tap(kh, kw), preferred_element_type=jnp.float32)
        conv_out = part if conv_out is None else conv_out + part
    stored_ref[...] = conv_out.astype(jnp.bfloat16)
    real = plan.real_rows()
    means, deviations = [], []
    for group in range(plan.groups):
        values = jnp.where(real, conv_out[:, group * LANES : (group + 1) * LANES], 0.0)
        mean = jnp.sum(values, axis=0, keepdims=True) / plan.count
        centred = jnp.where(real, values - mean, 0.0)
        means.append(mean)
        deviations.append(jnp.sqrt(jnp.sum(centred * centred, axis=0, keepdims=True) / plan.count))
    packed_ref[...] = jnp.concatenate(means + deviations, axis=0)


def exchange(plan, packed):
    copies = jnp.broadcast_to(packed.astype(jnp.float16), (plan.members,) + packed.shape)
    return lax.all_to_all(copies, "replica", 0, 0).astype(jnp.float32)


def join(plan, gathered, gain, bias):
    groups = plan.groups
    means, deviations = gathered[:, :groups], gathered[:, groups:]
    mean = jnp.sum(means, axis=0) / plan.members
    apart = means - mean[None]
    var = jnp.sum(deviations * deviations + apart * apart, axis=0) / plan.members
    scale = gain * lax.rsqrt(var + EPS)
    return scale, bias - mean * scale


def normalize_into(plan, stored_ref, scale, offset, write):
    real = plan.real_rows()
    for group in range(plan.groups):
        lanes = slice(group * LANES, (group + 1) * LANES)
        values = stored_ref[:, lanes].astype(jnp.float32) * scale[group : group + 1] + offset[group : group + 1]
        write(lanes, jnp.where(real, jnp.maximum(values, 0.0), 0.0).astype(jnp.bfloat16))


def in_vmem(value):
    return pltpu.with_memory_space_constraint(value, pltpu.VMEM)


def in_hbm(value):
    return pltpu.with_memory_space_constraint(value, pltpu.HBM)


def fetch_taps(kernel_hbm, taps, place, sems):
    return [
        pltpu.make_async_copy(kernel_hbm.at[kh, kw], place(i), sems.at[i]) for i, (kh, kw) in enumerate(taps)
    ]


def layer_outputs(plan):
    return [
        pltpu.VMEM((plan.rows, plan.channels), jnp.bfloat16),
        pltpu.VMEM((2 * plan.groups, LANES), jnp.float32),
    ]


def column(kernel):
    return pltpu.VMEM((3,) + kernel.shape[2:], kernel.dtype)


def padded_scratch(plan):
    return pltpu.VMEM((3, plan.rows + 2 * plan.line, plan.channels), jnp.bfloat16)


WHOLE = pl.BlockSpec(memory_space=pltpu.VMEM)
OUTSIDE = pl.BlockSpec(memory_space=pltpu.HBM)
PARAMS = pltpu.CompilerParams(vmem_limit_bytes=32 << 20)


def conv_layer(plan, body, operands, middle, kernel, following):
    ahead = [] if following is None else [following]

    def run(*refs):
        ins, refs = refs[: len(operands)], refs[len(operands) :]
        middle_ref, kernel_hbm, refs = refs[0], refs[1], refs[2:]
        next_hbm, refs = refs[: len(ahead)], refs[len(ahead) :]
        stored_ref, packed_ref, refs = refs[0], refs[1], refs[2:]
        next_middle, refs = refs[: len(ahead)], refs[len(ahead) :]
        padded, sides, sems, next_sems = refs
        copies = fetch_taps(kernel_hbm, SIDES, lambda i: sides.at[i], sems)
        for source, target in zip(next_hbm, next_middle):
            copies += fetch_taps(source, MIDDLE, lambda i: target.at[i], next_sems)
        for copy in copies:
            copy.start()
        zero_borders(plan, padded)
        body(padded, *ins)
        fill_shifted(plan, padded)

        def tap(kh, kw):
            if kw == 1:
                return middle_ref[kh]
            place = SIDES.index((kh, kw))
            copies[place].wait()
            return sides[place]

        convolve_and_measure(plan, padded, tap, stored_ref, packed_ref)
        for copy in copies[len(SIDES) :]:
            copy.wait()

    return pl.pallas_call(
        run,
        in_specs=[WHOLE] * (len(operands) + 1) + [OUTSIDE] * (1 + len(ahead)),
        out_specs=[WHOLE] * (2 + len(ahead)),
        out_shape=layer_outputs(plan) + [column(kernel) for kernel in ahead],
        scratch_shapes=[
            padded_scratch(plan),
            pltpu.VMEM((len(SIDES),) + kernel.shape[2:], kernel.dtype),
            pltpu.SemaphoreType.DMA((len(SIDES),)),
            pltpu.SemaphoreType.DMA((len(MIDDLE),)),
        ],
        compiler_params=PARAMS,
    )(*operands, in_vmem(middle), in_hbm(kernel), *map(in_hbm, ahead))


def inner(plan):
    return pl.ds(plan.line, plan.rows)


def spread_lines(plan, maps_ref, write):
    real = plan.width * plan.images
    blank = jnp.zeros((plan.line - real, plan.channels), jnp.bfloat16)
    for row in range(plan.height):
        write(row * plan.line, maps_ref[row].reshape(real, plan.channels))
        write(row * plan.line + real, blank)


def opening_layer(plan, maps, kernel, following):
    def run(maps_hbm, kernel_hbm, next_hbm, stored_ref, packed_ref, next_middle, *scratch):
        maps_vmem, map_sem, padded, filters, sems, next_sems = scratch
        fetch = pltpu.make_async_copy(maps_hbm, maps_vmem, map_sem)
        fetch.start()
        copies = fetch_taps(kernel_hbm, MIDDLE + SIDES, lambda i: filters.at[i], sems)
        ahead = fetch_taps(next_hbm, MIDDLE, lambda i: next_middle.at[i], next_sems)
        for copy in copies[: len(MIDDLE)]:
            copy.start()
        zero_borders(plan, padded)
        fetch.wait()
        for copy in copies[len(MIDDLE) :] + ahead:
            copy.start()

        def write(start, rows):
            padded[1, pl.ds(plan.line + start, rows.shape[0]), :] = rows

        spread_lines(plan, maps_vmem, write)
        fill_shifted(plan, padded)

        def tap(kh, kw):
            place = (MIDDLE + SIDES).index((kh, kw))
            copies[place].wait()
            return filters[place]

        convolve_and_measure(plan, padded, tap, stored_ref, packed_ref)
        for copy in ahead:
            copy.wait()

    return pl.pallas_call(
        run,
        in_specs=[OUTSIDE] * 3,
        out_specs=[WHOLE] * 3,
        out_shape=layer_outputs(plan) + [column(following)],
        scratch_shapes=[
            pltpu.VMEM(maps.shape, maps.dtype),
            pltpu.SemaphoreType.DMA(()),
            padded_scratch(plan),
            pltpu.VMEM((9,) + kernel.shape[2:], kernel.dtype),
            pltpu.SemaphoreType.DMA((9,)),
            pltpu.SemaphoreType.DMA((len(MIDDLE),)),
        ],
        compiler_params=PARAMS,
    )(in_hbm(maps), in_hbm(kernel), in_hbm(following))


def layer_of_stored(plan, stored, gathered, gain, bias, middle, kernel, following):
    def body(padded, stored_ref, gathered_ref, gain_ref, bias_ref):
        scale, offset = join(plan, gathered_ref[...], gain_ref[...], bias_ref[...])

        def write(lanes, values):
            padded[1, inner(plan), lanes] = values

        normalize_into(plan, stored_ref, scale, offset, write)

    return conv_layer(plan, body, [in_vmem(stored), gathered, gain, bias], middle, kernel, following)


def layer_of_moved(plan, stored, terms, maps, is_first, middle, kernel, following):
    def body(padded, stored_ref, terms_ref, maps_ref, first_ref):
        first = jnp.broadcast_to(first_ref[...], (plan.rows, LANES)) > 0.5

        def write(lanes, values):
            arrived = padded[1, inner(plan), lanes]
            padded[1, inner(plan), lanes] = jnp.where(first, arrived, values)

        def write_line(start, rows):
            padded[1, pl.ds(plan.line + start, rows.shape[0]), :] = rows

        spread_lines(plan, maps_ref, write_line)
        terms = terms_ref[...]
        normalize_into(plan, stored_ref, terms[: plan.groups], terms[plan.groups :], write)

    operands = [in_vmem(stored), terms, in_vmem(maps), is_first]
    return conv_layer(plan, body, operands, middle, kernel, following)


def finish(plan, stored, terms, gathered, gain, bias):
    shape = (TICKS, plan.height, plan.width, plan.images, plan.channels)

    def run(*refs):
        out_ref = refs[-1]
        for tick in range(TICKS):

            def write(lanes, values, tick=tick):
                for row in range(plan.height):
                    line = values[row * plan.line : row * plan.line + plan.width * plan.images]
                    out_ref[tick, row, :, :, lanes] = line.reshape(plan.width, plan.images, LANES)

            if tick + 1 < TICKS:
                known = refs[TICKS + tick][...]
                scale, offset = known[: plan.groups], known[plan.groups :]
            else:
                scale, offset = join(plan, *(ref[...] for ref in refs[2 * TICKS - 1 : -1]))
            normalize_into(plan, refs[tick], scale, offset, write)

    operands = [in_vmem(value) for value in stored] + terms + [gathered, gain, bias]
    return pl.pallas_call(
        run,
        in_specs=[WHOLE] * len(operands),
        out_specs=WHOLE,
        out_shape=pltpu.HBM(shape, jnp.bfloat16),
        compiler_params=PARAMS,
    )(*operands)


def from_behind(value, axis):
    pairs = [(i, i + 1) for i in range(lax.axis_size(axis) - 1)]
    return lax.ppermute(value, axis, pairs)


def body(
    pending_section_entries,
    arriving_microsets,
    opening_filter_kernel,
    closing_filter_kernel,
    stretch_factors,
    shift_terms,
):
    _, images, height, width, channels = pending_section_entries.shape
    plan = Plan(images, height, width, channels, lax.axis_size("replica"))
    first_kernel = opening_filter_kernel[0]
    second_kernel = closing_filter_kernel[0]
    is_first = jnp.broadcast_to((lax.axis_index("section") == 0).astype(jnp.float32), (1, LANES))
    order = (1, 2, 0, 3)
    maps = jnp.transpose(pending_section_entries[0], order)
    stored, packed, middle = opening_layer(plan, maps, first_kernel, second_kernel)
    kept, kept_terms = [], []
    for tick in range(TICKS):
        gathered = exchange(plan, packed)
        if tick == 0:
            gathered, gains, biases = lax.optimization_barrier((gathered, stretch_factors, shift_terms))
            gain = gains[0].reshape(2, plan.groups, LANES)
            bias = biases[0].reshape(2, plan.groups, LANES)
        last = tick + 1 == TICKS
        stored, packed, *middle = layer_of_stored(
            plan, stored, gathered, gain[0], bias[0], middle, second_kernel, None if last else first_kernel
        )
        kept.append(stored)
        if last:
            break
        moved = from_behind(stored, "section")
        terms = jnp.concatenate(join(plan, exchange(plan, packed), gain[1], bias[1]), axis=0)
        kept_terms.append(terms)
        terms = from_behind(terms, "section")
        arriving = jnp.transpose(arriving_microsets[tick], order)
        stored, packed, middle = layer_of_moved(
            plan, moved, terms, arriving, is_first, middle[0], first_kernel, second_kernel
        )
    result = finish(plan, kept, kept_terms, exchange(plan, packed), gain[1], bias[1])
    return jnp.transpose(result, (0, 3, 1, 2, 4))[None]


def solution(mesh):
    in_specs = (
        P("section", "replica", None, None, None),
        P(None, "replica", None, None, None),
        P("section", None, None, None, None),
        P("section", None, None, None, None),
        P("section", None, None),
        P("section", None, None),
    )
    out_specs = P("section", None, "replica", None, None, None)
    return jax.shard_map(body, mesh=mesh, in_specs=in_specs, out_specs=out_specs, check_vma=False)
```

```python
import jax
import jax.numpy as jnp
from jax import lax
from jax.experimental import pallas as pl
from jax.experimental.pallas import tpu as pltpu
from jax.sharding import PartitionSpec as P

TICKS = 2
LANES = 128
EPS = 1e-05


class Plan:
    def __init__(self, images, height, width, channels, members):
        self.images, self.height, self.width, self.channels = images, height, width, channels
        self.members = members
        self.wide = 16
        self.line = self.wide * images
        self.rows = height * self.line
        self.groups = channels // LANES
        self.count = images * height * width

    def real_rows(self):
        row = lax.broadcasted_iota(jnp.int32, (self.rows, LANES), 0)
        return row % self.line < self.width * self.images


def fill_shifted(plan, padded):
    line, rows, step = plan.line, plan.rows, plan.images
    padded[0, pl.ds(line, rows), :] = padded[1, pl.ds(line - step, rows), :]
    padded[2, pl.ds(line, rows), :] = padded[1, pl.ds(line + step, rows), :]


def zero_borders(plan, padded):
    border = jnp.zeros((plan.line, plan.channels), jnp.bfloat16)
    for shift in range(3):
        padded[shift, pl.ds(0, plan.line), :] = border
        padded[shift, pl.ds(plan.line + plan.rows, plan.line), :] = border


TAPS = [(0, 1), (1, 1), (2, 1), (0, 0), (1, 0), (2, 0), (0, 2), (1, 2), (2, 2)]
OPENING_AHEAD = 3
CLOSING_AHEAD = 4


def convolve_and_measure(plan, padded, tap, stored_ref, packed_ref):
    conv_out = None
    for kh, kw in TAPS:
        shifted = padded[kw, pl.ds(kh * plan.line, plan.rows), :]
        part = jnp.dot(shifted, tap(kh, kw), preferred_element_type=jnp.float32)
        conv_out = part if conv_out is None else conv_out + part
    stored_ref[...] = conv_out.astype(jnp.bfloat16)
    real = plan.real_rows()
    means, deviations = [], []
    for group in range(plan.groups):
        values = jnp.where(real, conv_out[:, group * LANES : (group + 1) * LANES], 0.0)
        mean = jnp.sum(values, axis=0, keepdims=True) / plan.count
        centred = jnp.where(real, values - mean, 0.0)
        means.append(mean)
        deviations.append(jnp.sqrt(jnp.sum(centred * centred, axis=0, keepdims=True) / plan.count))
    packed_ref[...] = jnp.concatenate(means + deviations, axis=0)


def exchange(plan, packed):
    copies = jnp.broadcast_to(packed.astype(jnp.float16), (plan.members,) + packed.shape)
    return lax.all_to_all(copies, "replica", 0, 0).astype(jnp.float32)


def join(plan, gathered, gain, bias):
    groups = plan.groups
    means, deviations = gathered[:, :groups], gathered[:, groups:]
    mean = jnp.sum(means, axis=0) / plan.members
    apart = means - mean[None]
    var = jnp.sum(deviations * deviations + apart * apart, axis=0) / plan.members
    scale = gain * lax.rsqrt(var + EPS)
    return scale, bias - mean * scale


def normalize_into(plan, stored_ref, scale, offset, write):
    real = plan.real_rows()
    for group in range(plan.groups):
        lanes = slice(group * LANES, (group + 1) * LANES)
        values = stored_ref[:, lanes].astype(jnp.float32) * scale[group : group + 1] + offset[group : group + 1]
        write(lanes, jnp.where(real, jnp.maximum(values, 0.0), 0.0).astype(jnp.bfloat16))


def in_vmem(value):
    return pltpu.with_memory_space_constraint(value, pltpu.VMEM)


def in_hbm(value):
    return pltpu.with_memory_space_constraint(value, pltpu.HBM)


def fetch_taps(kernel_hbm, taps, place, sems):
    return [
        pltpu.make_async_copy(kernel_hbm.at[kh, kw], place(i), sems.at[i]) for i, (kh, kw) in enumerate(taps)
    ]


def layer_outputs(plan):
    return [
        pltpu.VMEM((plan.rows, plan.channels), jnp.bfloat16),
        pltpu.VMEM((2 * plan.groups, LANES), jnp.float32),
    ]


def filters_in_vmem(taps, kernel):
    return pltpu.VMEM((len(taps),) + kernel.shape[2:], kernel.dtype)


def padded_scratch(plan):
    return pltpu.VMEM((3, plan.rows + 2 * plan.line, plan.channels), jnp.bfloat16)


WHOLE = pl.BlockSpec(memory_space=pltpu.VMEM)
OUTSIDE = pl.BlockSpec(memory_space=pltpu.HBM)
PARAMS = pltpu.CompilerParams(vmem_limit_bytes=32 << 20)


def conv_layer(plan, body, operands, early, kernel, following, count):
    ahead = [] if following is None else [following]
    first, late, upcoming = TAPS[: early.shape[0]], TAPS[early.shape[0] :], TAPS[:count]

    def run(*refs):
        ins, refs = refs[: len(operands)], refs[len(operands) :]
        early_ref, kernel_hbm, refs = refs[0], refs[1], refs[2:]
        next_hbm, refs = refs[: len(ahead)], refs[len(ahead) :]
        stored_ref, packed_ref, refs = refs[0], refs[1], refs[2:]
        next_early, refs = refs[: len(ahead)], refs[len(ahead) :]
        padded, sides, sems, next_sems = refs
        copies = fetch_taps(kernel_hbm, late, lambda i: sides.at[i], sems)
        for source, target in zip(next_hbm, next_early):
            copies += fetch_taps(source, upcoming, lambda i: target.at[i], next_sems)
        for copy in copies:
            copy.start()
        zero_borders(plan, padded)
        body(padded, *ins)
        fill_shifted(plan, padded)

        def tap(kh, kw):
            if (kh, kw) in first:
                return early_ref[first.index((kh, kw))]
            place = late.index((kh, kw))
            copies[place].wait()
            return sides[place]

        convolve_and_measure(plan, padded, tap, stored_ref, packed_ref)
        for copy in copies[len(late) :]:
            copy.wait()

    return pl.pallas_call(
        run,
        in_specs=[WHOLE] * (len(operands) + 1) + [OUTSIDE] * (1 + len(ahead)),
        out_specs=[WHOLE] * (2 + len(ahead)),
        out_shape=layer_outputs(plan) + [filters_in_vmem(upcoming, kernel) for kernel in ahead],
        scratch_shapes=[
            padded_scratch(plan),
            filters_in_vmem(late, kernel),
            pltpu.SemaphoreType.DMA((len(late),)),
            pltpu.SemaphoreType.DMA((max(count, 1),)),
        ],
        compiler_params=PARAMS,
    )(*operands, in_vmem(early), in_hbm(kernel), *map(in_hbm, ahead))


def inner(plan):
    return pl.ds(plan.line, plan.rows)


def spread_lines(plan, maps_ref, write):
    real = plan.width * plan.images
    blank = jnp.zeros((plan.line - real, plan.channels), jnp.bfloat16)
    for row in range(plan.height):
        write(row * plan.line, maps_ref[row].reshape(real, plan.channels))
        write(row * plan.line + real, blank)


def opening_layer(plan, maps, kernel, following, count):
    def run(maps_hbm, kernel_hbm, next_hbm, stored_ref, packed_ref, next_early, *scratch):
        maps_vmem, map_sem, padded, filters, sems, next_sems = scratch
        fetch = pltpu.make_async_copy(maps_hbm, maps_vmem, map_sem)
        fetch.start()
        copies = fetch_taps(kernel_hbm, TAPS, lambda i: filters.at[i], sems)
        ahead = fetch_taps(next_hbm, TAPS[:count], lambda i: next_early.at[i], next_sems)
        for copy in copies[:3]:
            copy.start()
        zero_borders(plan, padded)
        fetch.wait()
        for copy in copies[3:] + ahead:
            copy.start()

        def write(start, rows):
            padded[1, pl.ds(plan.line + start, rows.shape[0]), :] = rows

        spread_lines(plan, maps_vmem, write)
        fill_shifted(plan, padded)

        def tap(kh, kw):
            place = TAPS.index((kh, kw))
            copies[place].wait()
            return filters[place]

        convolve_and_measure(plan, padded, tap, stored_ref, packed_ref)
        for copy in ahead:
            copy.wait()

    return pl.pallas_call(
        run,
        in_specs=[OUTSIDE] * 3,
        out_specs=[WHOLE] * 3,
        out_shape=layer_outputs(plan) + [filters_in_vmem(TAPS[:count], following)],
        scratch_shapes=[
            pltpu.VMEM(maps.shape, maps.dtype),
            pltpu.SemaphoreType.DMA(()),
            padded_scratch(plan),
            filters_in_vmem(TAPS, kernel),
            pltpu.SemaphoreType.DMA((len(TAPS),)),
            pltpu.SemaphoreType.DMA((count,)),
        ],
        compiler_params=PARAMS,
    )(in_hbm(maps), in_hbm(kernel), in_hbm(following))


def layer_of_stored(plan, stored, gathered, gain, bias, early, kernel, following, count):
    def body(padded, stored_ref, gathered_ref, gain_ref, bias_ref):
        scale, offset = join(plan, gathered_ref[...], gain_ref[...], bias_ref[...])

        def write(lanes, values):
            padded[1, inner(plan), lanes] = values

        normalize_into(plan, stored_ref, scale, offset, write)

    return conv_layer(plan, body, [in_vmem(stored), gathered, gain, bias], early, kernel, following, count)


def layer_of_moved(plan, stored, terms, maps, is_first, early, kernel, following, count):
    def body(padded, stored_ref, terms_ref, maps_ref, first_ref):
        first = jnp.broadcast_to(first_ref[...], (plan.rows, LANES)) > 0.5

        def write(lanes, values):
            arrived = padded[1, inner(plan), lanes]
            padded[1, inner(plan), lanes] = jnp.where(first, arrived, values)

        def write_line(start, rows):
            padded[1, pl.ds(plan.line + start, rows.shape[0]), :] = rows

        spread_lines(plan, maps_ref, write_line)
        terms = terms_ref[...]
        normalize_into(plan, stored_ref, terms[: plan.groups], terms[plan.groups :], write)

    operands = [in_vmem(stored), terms, in_vmem(maps), is_first]
    return conv_layer(plan, body, operands, early, kernel, following, count)


def finish(plan, stored, terms, gathered, gain, bias):
    shape = (TICKS, plan.height, plan.width, plan.images, plan.channels)

    def run(*refs):
        *refs, out_hbm, out_ref, sems = refs
        copies = []
        for tick in range(TICKS):

            def write(lanes, values, tick=tick):
                for row in range(plan.height):
                    line = values[row * plan.line : row * plan.line + plan.width * plan.images]
                    out_ref[tick, row, :, :, lanes] = line.reshape(plan.width, plan.images, LANES)

            if tick + 1 < TICKS:
                known = refs[TICKS + tick][...]
                scale, offset = known[: plan.groups], known[plan.groups :]
            else:
                scale, offset = join(plan, *(ref[...] for ref in refs[2 * TICKS - 1 :]))
            normalize_into(plan, refs[tick], scale, offset, write)
            copies.append(pltpu.make_async_copy(out_ref.at[tick], out_hbm.at[tick], sems.at[tick]))
            copies[-1].start()
        for copy in copies:
            copy.wait()

    operands = [in_vmem(value) for value in stored] + terms + [gathered, gain, bias]
    return pl.pallas_call(
        run,
        in_specs=[WHOLE] * len(operands),
        out_specs=OUTSIDE,
        out_shape=pltpu.HBM(shape, jnp.bfloat16),
        scratch_shapes=[pltpu.VMEM(shape, jnp.bfloat16), pltpu.SemaphoreType.DMA((TICKS,))],
        compiler_params=PARAMS,
    )(*operands)


def from_behind(value, axis):
    length = lax.axis_size(axis)
    return lax.ppermute(value, axis, [(i, (i + 1) % length) for i in range(length)])


def body(
    pending_section_entries,
    arriving_microsets,
    opening_filter_kernel,
    closing_filter_kernel,
    stretch_factors,
    shift_terms,
):
    _, images, height, width, channels = pending_section_entries.shape
    plan = Plan(images, height, width, channels, lax.axis_size("replica"))
    first_kernel = opening_filter_kernel[0]
    second_kernel = closing_filter_kernel[0]
    is_first = jnp.broadcast_to((lax.axis_index("section") == 0).astype(jnp.float32), (1, LANES))
    order = (1, 2, 0, 3)
    maps = jnp.transpose(pending_section_entries[0], order)
    stored, packed, early = opening_layer(plan, maps, first_kernel, second_kernel, CLOSING_AHEAD)
    kept, kept_terms = [], []
    for tick in range(TICKS):
        gathered = exchange(plan, packed)
        if tick == 0:
            gathered, gains, biases = lax.optimization_barrier((gathered, stretch_factors, shift_terms))
            gain = gains[0].reshape(2, plan.groups, LANES)
            bias = biases[0].reshape(2, plan.groups, LANES)
        last = tick + 1 == TICKS
        ahead = (None, 0) if last else (first_kernel, OPENING_AHEAD)
        stored, packed, *early = layer_of_stored(
            plan, stored, gathered, gain[0], bias[0], early, second_kernel, *ahead
        )
        kept.append(stored)
        if last:
            break
        moved = from_behind(stored, "section")
        terms = jnp.concatenate(join(plan, exchange(plan, packed), gain[1], bias[1]), axis=0)
        kept_terms.append(terms)
        terms = from_behind(terms, "section")
        arriving = jnp.transpose(arriving_microsets[tick], order)
        ahead = (second_kernel, CLOSING_AHEAD)
        stored, packed, early = layer_of_moved(
            plan, moved, terms, arriving, is_first, early[0], first_kernel, *ahead
        )
    result = finish(plan, kept, kept_terms, exchange(plan, packed), gain[1], bias[1])
    return jnp.transpose(result, (0, 3, 1, 2, 4))[None]


def solution(mesh):
    in_specs = (
        P("section", "replica", None, None, None),
        P(None, "replica", None, None, None),
        P("section", None, None, None, None),
        P("section", None, None, None, None),
        P("section", None, None),
        P("section", None, None),
    )
    out_specs = P("section", None, "replica", None, None, None)
    return jax.shard_map(body, mesh=mesh, in_specs=in_specs, out_specs=out_specs, check_vma=False)
```

```python
import jax
import jax.numpy as jnp
from jax import lax
from jax.experimental import pallas as pl
from jax.experimental.pallas import tpu as pltpu
from jax.sharding import PartitionSpec as P

TICKS = 2
LANES = 128
EPS = 1e-05


class Plan:
    def __init__(self, images, height, width, channels, members):
        self.images, self.height, self.width, self.channels = images, height, width, channels
        self.members = members
        self.wide = 16
        self.line = self.wide * images
        self.rows = height * self.line
        self.groups = channels // LANES
        self.count = images * height * width

    def real_rows(self):
        row = lax.broadcasted_iota(jnp.int32, (self.rows, LANES), 0)
        return row % self.line < self.width * self.images


def fill_shifted(plan, padded):
    line, rows, step = plan.line, plan.rows, plan.images
    padded[0, pl.ds(line, rows), :] = padded[1, pl.ds(line - step, rows), :]
    padded[2, pl.ds(line, rows), :] = padded[1, pl.ds(line + step, rows), :]


def zero_borders(plan, padded):
    border = jnp.zeros((plan.line, plan.channels), jnp.bfloat16)
    for shift in range(3):
        padded[shift, pl.ds(0, plan.line), :] = border
        padded[shift, pl.ds(plan.line + plan.rows, plan.line), :] = border


TAPS = [(0, 1), (1, 1), (2, 1), (0, 0), (1, 0), (2, 0), (0, 2), (1, 2), (2, 2)]
OPENING_AHEAD = 4
CLOSING_AHEAD = 4


def convolve_and_measure(plan, padded, tap, stored_ref, packed_ref):
    conv_out = None
    for kh, kw in TAPS:
        shifted = padded[kw, pl.ds(kh * plan.line, plan.rows), :]
        part = jnp.dot(shifted, tap(kh, kw), preferred_element_type=jnp.float32)
        conv_out = part if conv_out is None else conv_out + part
    stored_ref[...] = conv_out.astype(jnp.bfloat16)
    real = plan.real_rows()
    means, deviations = [], []
    for group in range(plan.groups):
        values = jnp.where(real, conv_out[:, group * LANES : (group + 1) * LANES], 0.0)
        mean = jnp.sum(values, axis=0, keepdims=True) / plan.count
        centred = jnp.where(real, values - mean, 0.0)
        means.append(mean)
        deviations.append(jnp.sqrt(jnp.sum(centred * centred, axis=0, keepdims=True) / plan.count))
    packed_ref[...] = jnp.concatenate(means + deviations, axis=0)


def exchange(plan, packed):
    copies = jnp.broadcast_to(packed.astype(jnp.float16), (plan.members,) + packed.shape)
    return lax.all_to_all(copies, "replica", 0, 0).astype(jnp.float32)


def join(plan, gathered, gain, bias):
    groups = plan.groups
    means, deviations = gathered[:, :groups], gathered[:, groups:]
    mean = jnp.sum(means, axis=0) / plan.members
    apart = means - mean[None]
    var = jnp.sum(deviations * deviations + apart * apart, axis=0) / plan.members
    scale = gain * lax.rsqrt(var + EPS)
    return scale, bias - mean * scale


def normalize_into(plan, stored_ref, scale, offset, write):
    real = plan.real_rows()
    for group in range(plan.groups):
        lanes = slice(group * LANES, (group + 1) * LANES)
        values = stored_ref[:, lanes].astype(jnp.float32) * scale[group : group + 1] + offset[group : group + 1]
        write(lanes, jnp.where(real, jnp.maximum(values, 0.0), 0.0).astype(jnp.bfloat16))


def in_vmem(value):
    return pltpu.with_memory_space_constraint(value, pltpu.VMEM)


def in_hbm(value):
    return pltpu.with_memory_space_constraint(value, pltpu.HBM)


def fetch_taps(kernel_hbm, taps, place, sems):
    return [
        pltpu.make_async_copy(kernel_hbm.at[kh, kw], place(i), sems.at[i]) for i, (kh, kw) in enumerate(taps)
    ]


def layer_outputs(plan):
    return [
        pltpu.VMEM((plan.rows, plan.channels), jnp.bfloat16),
        pltpu.VMEM((2 * plan.groups, LANES), jnp.float32),
    ]


def filters_in_vmem(taps, kernel):
    return pltpu.VMEM((len(taps),) + kernel.shape[2:], kernel.dtype)


def padded_scratch(plan):
    return pltpu.VMEM((3, plan.rows + 2 * plan.line, plan.channels), jnp.bfloat16)


WHOLE = pl.BlockSpec(memory_space=pltpu.VMEM)
OUTSIDE = pl.BlockSpec(memory_space=pltpu.HBM)
PARAMS = pltpu.CompilerParams(vmem_limit_bytes=32 << 20)


def conv_layer(plan, body, operands, early, kernel, following, count):
    ahead = [] if following is None else [following]
    first, late, upcoming = TAPS[: early.shape[0]], TAPS[early.shape[0] :], TAPS[:count]

    def run(*refs):
        ins, refs = refs[: len(operands)], refs[len(operands) :]
        early_ref, kernel_hbm, refs = refs[0], refs[1], refs[2:]
        next_hbm, refs = refs[: len(ahead)], refs[len(ahead) :]
        stored_ref, packed_ref, refs = refs[0], refs[1], refs[2:]
        next_early, refs = refs[: len(ahead)], refs[len(ahead) :]
        padded, sides, sems, next_sems = refs
        copies = fetch_taps(kernel_hbm, late, lambda i: sides.at[i], sems)
        for source, target in zip(next_hbm, next_early):
            copies += fetch_taps(source, upcoming, lambda i: target.at[i], next_sems)
        for copy in copies:
            copy.start()
        zero_borders(plan, padded)
        body(padded, *ins)
        fill_shifted(plan, padded)

        def tap(kh, kw):
            if (kh, kw) in first:
                return early_ref[first.index((kh, kw))]
            place = late.index((kh, kw))
            copies[place].wait()
            return sides[place]

        convolve_and_measure(plan, padded, tap, stored_ref, packed_ref)
        for copy in copies[len(late) :]:
            copy.wait()

    return pl.pallas_call(
        run,
        in_specs=[WHOLE] * (len(operands) + 1) + [OUTSIDE] * (1 + len(ahead)),
        out_specs=[WHOLE] * (2 + len(ahead)),
        out_shape=layer_outputs(plan) + [filters_in_vmem(upcoming, kernel) for kernel in ahead],
        scratch_shapes=[
            padded_scratch(plan),
            filters_in_vmem(late, kernel),
            pltpu.SemaphoreType.DMA((len(late),)),
            pltpu.SemaphoreType.DMA((max(count, 1),)),
        ],
        compiler_params=PARAMS,
    )(*operands, in_vmem(early), in_hbm(kernel), *map(in_hbm, ahead))


def inner(plan):
    return pl.ds(plan.line, plan.rows)


def spread_lines(plan, maps_ref, write):
    real = plan.width * plan.images
    blank = jnp.zeros((plan.line - real, plan.channels), jnp.bfloat16)
    for row in range(plan.height):
        write(row * plan.line, maps_ref[row].reshape(real, plan.channels))
        write(row * plan.line + real, blank)


def opening_layer(plan, maps, kernel, following, count):
    def run(maps_hbm, kernel_hbm, next_hbm, stored_ref, packed_ref, next_early, *scratch):
        maps_vmem, map_sem, padded, filters, sems, next_sems = scratch
        fetch = pltpu.make_async_copy(maps_hbm, maps_vmem, map_sem)
        fetch.start()
        copies = fetch_taps(kernel_hbm, TAPS, lambda i: filters.at[i], sems)
        ahead = fetch_taps(next_hbm, TAPS[:count], lambda i: next_early.at[i], next_sems)
        for copy in copies[:3]:
            copy.start()
        zero_borders(plan, padded)
        fetch.wait()
        for copy in copies[3:] + ahead:
            copy.start()

        def write(start, rows):
            padded[1, pl.ds(plan.line + start, rows.shape[0]), :] = rows

        spread_lines(plan, maps_vmem, write)
        fill_shifted(plan, padded)

        def tap(kh, kw):
            place = TAPS.index((kh, kw))
            copies[place].wait()
            return filters[place]

        convolve_and_measure(plan, padded, tap, stored_ref, packed_ref)
        for copy in ahead:
            copy.wait()

    return pl.pallas_call(
        run,
        in_specs=[OUTSIDE] * 3,
        out_specs=[WHOLE] * 3,
        out_shape=layer_outputs(plan) + [filters_in_vmem(TAPS[:count], following)],
        scratch_shapes=[
            pltpu.VMEM(maps.shape, maps.dtype),
            pltpu.SemaphoreType.DMA(()),
            padded_scratch(plan),
            filters_in_vmem(TAPS, kernel),
            pltpu.SemaphoreType.DMA((len(TAPS),)),
            pltpu.SemaphoreType.DMA((count,)),
        ],
        compiler_params=PARAMS,
    )(in_hbm(maps), in_hbm(kernel), in_hbm(following))


def layer_of_stored(plan, stored, gathered, gain, bias, early, kernel, following, count):
    def body(padded, stored_ref, gathered_ref, gain_ref, bias_ref):
        scale, offset = join(plan, gathered_ref[...], gain_ref[...], bias_ref[...])

        def write(lanes, values):
            padded[1, inner(plan), lanes] = values

        normalize_into(plan, stored_ref, scale, offset, write)

    return conv_layer(plan, body, [in_vmem(stored), gathered, gain, bias], early, kernel, following, count)


def layer_of_moved(plan, stored, terms, maps, is_first, early, kernel, following, count):
    def body(padded, stored_ref, terms_ref, maps_ref, first_ref):
        first = jnp.broadcast_to(first_ref[...], (plan.rows, LANES)) > 0.5

        def write(lanes, values):
            arrived = padded[1, inner(plan), lanes]
            padded[1, inner(plan), lanes] = jnp.where(first, arrived, values)

        def write_line(start, rows):
            padded[1, pl.ds(plan.line + start, rows.shape[0]), :] = rows

        spread_lines(plan, maps_ref, write_line)
        terms = terms_ref[...]
        normalize_into(plan, stored_ref, terms[: plan.groups], terms[plan.groups :], write)

    operands = [in_vmem(stored), terms, in_vmem(maps), is_first]
    return conv_layer(plan, body, operands, early, kernel, following, count)


def finish(plan, stored, terms, gathered, gain, bias):
    shape = (TICKS, plan.height, plan.width, plan.images, plan.channels)

    def run(*refs):
        *refs, out_hbm, out_ref, sems = refs
        copies = []
        for tick in range(TICKS):

            def write(lanes, values, tick=tick):
                for row in range(plan.height):
                    line = values[row * plan.line : row * plan.line + plan.width * plan.images]
                    out_ref[tick, row, :, :, lanes] = line.reshape(plan.width, plan.images, LANES)

            if tick + 1 < TICKS:
                known = refs[TICKS + tick][...]
                scale, offset = known[: plan.groups], known[plan.groups :]
            else:
                scale, offset = join(plan, *(ref[...] for ref in refs[2 * TICKS - 1 :]))
            normalize_into(plan, refs[tick], scale, offset, write)
            copies.append(pltpu.make_async_copy(out_ref.at[tick], out_hbm.at[tick], sems.at[tick]))
            copies[-1].start()
        for copy in copies:
            copy.wait()

    operands = [in_vmem(value) for value in stored] + terms + [gathered, gain, bias]
    return pl.pallas_call(
        run,
        in_specs=[WHOLE] * len(operands),
        out_specs=OUTSIDE,
        out_shape=pltpu.HBM(shape, jnp.bfloat16),
        scratch_shapes=[pltpu.VMEM(shape, jnp.bfloat16), pltpu.SemaphoreType.DMA((TICKS,))],
        compiler_params=PARAMS,
    )(*operands)


def from_behind(value, axis):
    length = lax.axis_size(axis)
    return lax.ppermute(value, axis, [(i, (i + 1) % length) for i in range(length)])


def body(
    pending_section_entries,
    arriving_microsets,
    opening_filter_kernel,
    closing_filter_kernel,
    stretch_factors,
    shift_terms,
):
    _, images, height, width, channels = pending_section_entries.shape
    plan = Plan(images, height, width, channels, lax.axis_size("replica"))
    first_kernel = opening_filter_kernel[0]
    second_kernel = closing_filter_kernel[0]
    is_first = jnp.broadcast_to((lax.axis_index("section") == 0).astype(jnp.float32), (1, LANES))
    order = (1, 2, 0, 3)
    maps = jnp.transpose(pending_section_entries[0], order)
    stored, packed, early = opening_layer(plan, maps, first_kernel, second_kernel, CLOSING_AHEAD)
    kept, kept_terms = [], []
    for tick in range(TICKS):
        gathered = exchange(plan, packed)
        if tick == 0:
            gathered, gains, biases = lax.optimization_barrier((gathered, stretch_factors, shift_terms))
            gain = gains[0].reshape(2, plan.groups, LANES)
            bias = biases[0].reshape(2, plan.groups, LANES)
        last = tick + 1 == TICKS
        ahead = (None, 0) if last else (first_kernel, OPENING_AHEAD)
        stored, packed, *early = layer_of_stored(
            plan, stored, gathered, gain[0], bias[0], early, second_kernel, *ahead
        )
        kept.append(stored)
        if last:
            break
        moved = from_behind(stored, "section")
        terms = jnp.concatenate(join(plan, exchange(plan, packed), gain[1], bias[1]), axis=0)
        kept_terms.append(terms)
        terms = from_behind(terms, "section")
        arriving = jnp.transpose(arriving_microsets[tick], order)
        ahead = (second_kernel, CLOSING_AHEAD)
        stored, packed, early = layer_of_moved(
            plan, moved, terms, arriving, is_first, early[0], first_kernel, *ahead
        )
    result = finish(plan, kept, kept_terms, exchange(plan, packed), gain[1], bias[1])
    return jnp.transpose(result, (0, 3, 1, 2, 4))[None]


def solution(mesh):
    in_specs = (
        P("section", "replica", None, None, None),
        P(None, "replica", None, None, None),
        P("section", None, None, None, None),
        P("section", None, None, None, None),
        P("section", None, None),
        P("section", None, None),
    )
    out_specs = P("section", None, "replica", None, None, None)
    return jax.shard_map(body, mesh=mesh, in_specs=in_specs, out_specs=out_specs, check_vma=False)
```

```python
import jax
import jax.numpy as jnp
from jax import lax
from jax.experimental import pallas as pl
from jax.experimental.pallas import tpu as pltpu
from jax.sharding import PartitionSpec as P

TICKS = 2
LANES = 128
EPS = 1e-05


class Plan:
    def __init__(self, images, height, width, channels, members):
        self.images, self.height, self.width, self.channels = images, height, width, channels
        self.members = members
        self.wide = 16
        self.line = self.wide * images
        self.rows = height * self.line
        self.groups = channels // LANES
        self.count = images * height * width

    def real_rows(self):
        row = lax.broadcasted_iota(jnp.int32, (self.rows, LANES), 0)
        return row % self.line < self.width * self.images


def fill_shifted(plan, padded):
    line, rows, step = plan.line, plan.rows, plan.images
    padded[0, pl.ds(line, rows), :] = padded[1, pl.ds(line - step, rows), :]
    padded[2, pl.ds(line, rows), :] = padded[1, pl.ds(line + step, rows), :]


def zero_borders(plan, padded):
    border = jnp.zeros((plan.line, plan.channels), jnp.bfloat16)
    for shift in range(3):
        padded[shift, pl.ds(0, plan.line), :] = border
        padded[shift, pl.ds(plan.line + plan.rows, plan.line), :] = border


TAPS = [(0, 1), (1, 1), (2, 1), (0, 0), (1, 0), (2, 0), (0, 2), (1, 2), (2, 2)]
OPENING_AHEAD = 3.5
CLOSING_AHEAD = 4


def early_and_late(channels, count):
    early, late = [], []
    for place, (kh, kw) in enumerate(TAPS):
        split = int(channels * min(max(count - place, 0), 1))
        if split > 0:
            early.append((kh, kw, 0, split))
        if split < channels:
            late.append((kh, kw, split, channels - split))
    return early, late


def row_of(taps, place):
    return sum(size for _, _, _, size in taps[:place])


def convolve_and_measure(plan, padded, taps, filters_of, stored_ref, packed_ref):
    conv_out = None
    for tap in taps:
        kh, kw, channel, size = tap
        shifted = padded[kw, pl.ds(kh * plan.line, plan.rows), channel : channel + size]
        part = jnp.dot(shifted, filters_of(tap), preferred_element_type=jnp.float32)
        conv_out = part if conv_out is None else conv_out + part
    stored_ref[...] = conv_out.astype(jnp.bfloat16)
    real = plan.real_rows()
    means, deviations = [], []
    for group in range(plan.groups):
        values = jnp.where(real, conv_out[:, group * LANES : (group + 1) * LANES], 0.0)
        mean = jnp.sum(values, axis=0, keepdims=True) / plan.count
        centred = jnp.where(real, values - mean, 0.0)
        means.append(mean)
        deviations.append(jnp.sqrt(jnp.sum(centred * centred, axis=0, keepdims=True) / plan.count))
    packed_ref[...] = jnp.concatenate(means + deviations, axis=0)


def exchange(plan, packed):
    copies = jnp.broadcast_to(packed.astype(jnp.float16), (plan.members,) + packed.shape)
    return lax.all_to_all(copies, "replica", 0, 0).astype(jnp.float32)


def join(plan, gathered, gain, bias):
    groups = plan.groups
    means, deviations = gathered[:, :groups], gathered[:, groups:]
    mean = jnp.sum(means, axis=0) / plan.members
    apart = means - mean[None]
    var = jnp.sum(deviations * deviations + apart * apart, axis=0) / plan.members
    scale = gain * lax.rsqrt(var + EPS)
    return scale, bias - mean * scale


def normalize_into(plan, stored_ref, scale, offset, write):
    real = plan.real_rows()
    for group in range(plan.groups):
        lanes = slice(group * LANES, (group + 1) * LANES)
        values = stored_ref[:, lanes].astype(jnp.float32) * scale[group : group + 1] + offset[group : group + 1]
        write(lanes, jnp.where(real, jnp.maximum(values, 0.0), 0.0).astype(jnp.bfloat16))


def in_vmem(value):
    return pltpu.with_memory_space_constraint(value, pltpu.VMEM)


def in_hbm(value):
    return pltpu.with_memory_space_constraint(value, pltpu.HBM)


def fetch_taps(kernel_hbm, taps, target, sems):
    copies = []
    for place, (kh, kw, channel, size) in enumerate(taps):
        source = kernel_hbm.at[kh, kw, pl.ds(channel, size)]
        copies.append(pltpu.make_async_copy(source, target.at[pl.ds(row_of(taps, place), size)], sems.at[place]))
    return copies


def layer_outputs(plan):
    return [
        pltpu.VMEM((plan.rows, plan.channels), jnp.bfloat16),
        pltpu.VMEM((2 * plan.groups, LANES), jnp.float32),
    ]


def filters_in_vmem(taps, kernel):
    return pltpu.VMEM((row_of(taps, len(taps)), kernel.shape[3]), kernel.dtype)


def padded_scratch(plan):
    return pltpu.VMEM((3, plan.rows + 2 * plan.line, plan.channels), jnp.bfloat16)


WHOLE = pl.BlockSpec(memory_space=pltpu.VMEM)
OUTSIDE = pl.BlockSpec(memory_space=pltpu.HBM)
PARAMS = pltpu.CompilerParams(vmem_limit_bytes=32 << 20)


def conv_layer(plan, body, operands, early, kernel, following, count):
    ahead = [] if following is None else [following]
    first, late = early_and_late(plan.channels, early.shape[0] / plan.channels)
    upcoming, _ = early_and_late(plan.channels, count)

    def run(*refs):
        ins, refs = refs[: len(operands)], refs[len(operands) :]
        early_ref, kernel_hbm, refs = refs[0], refs[1], refs[2:]
        next_hbm, refs = refs[: len(ahead)], refs[len(ahead) :]
        stored_ref, packed_ref, refs = refs[0], refs[1], refs[2:]
        next_early, refs = refs[: len(ahead)], refs[len(ahead) :]
        padded, sides, sems, next_sems = refs
        copies = fetch_taps(kernel_hbm, late, sides, sems)
        for source, target in zip(next_hbm, next_early):
            copies += fetch_taps(source, upcoming, target, next_sems)
        for copy in copies:
            copy.start()
        zero_borders(plan, padded)
        body(padded, *ins)
        fill_shifted(plan, padded)

        def filters_of(tap):
            if tap in first:
                return early_ref[pl.ds(row_of(first, first.index(tap)), tap[3]), :]
            place = late.index(tap)
            copies[place].wait()
            return sides[pl.ds(row_of(late, place), tap[3]), :]

        convolve_and_measure(plan, padded, first + late, filters_of, stored_ref, packed_ref)
        for copy in copies[len(late) :]:
            copy.wait()

    return pl.pallas_call(
        run,
        in_specs=[WHOLE] * (len(operands) + 1) + [OUTSIDE] * (1 + len(ahead)),
        out_specs=[WHOLE] * (2 + len(ahead)),
        out_shape=layer_outputs(plan) + [filters_in_vmem(upcoming, kernel) for kernel in ahead],
        scratch_shapes=[
            padded_scratch(plan),
            filters_in_vmem(late, kernel),
            pltpu.SemaphoreType.DMA((len(late),)),
            pltpu.SemaphoreType.DMA((max(len(upcoming), 1),)),
        ],
        compiler_params=PARAMS,
    )(*operands, in_vmem(early), in_hbm(kernel), *map(in_hbm, ahead))


def inner(plan):
    return pl.ds(plan.line, plan.rows)


def spread_lines(plan, maps_ref, write):
    real = plan.width * plan.images
    blank = jnp.zeros((plan.line - real, plan.channels), jnp.bfloat16)
    for row in range(plan.height):
        write(row * plan.line, maps_ref[row].reshape(real, plan.channels))
        write(row * plan.line + real, blank)


def opening_layer(plan, maps, kernel, following, count):
    _, taps = early_and_late(plan.channels, 0)
    upcoming, _ = early_and_late(plan.channels, count)

    def run(maps_hbm, kernel_hbm, next_hbm, stored_ref, packed_ref, next_early, *scratch):
        maps_vmem, map_sem, padded, filters, sems, next_sems = scratch
        fetch = pltpu.make_async_copy(maps_hbm, maps_vmem, map_sem)
        fetch.start()
        copies = fetch_taps(kernel_hbm, taps, filters, sems)
        ahead = fetch_taps(next_hbm, upcoming, next_early, next_sems)
        for copy in copies[:3]:
            copy.start()
        zero_borders(plan, padded)
        fetch.wait()
        for copy in copies[3:] + ahead:
            copy.start()

        def write(start, rows):
            padded[1, pl.ds(plan.line + start, rows.shape[0]), :] = rows

        spread_lines(plan, maps_vmem, write)
        fill_shifted(plan, padded)

        def filters_of(tap):
            place = taps.index(tap)
            copies[place].wait()
            return filters[pl.ds(row_of(taps, place), tap[3]), :]

        convolve_and_measure(plan, padded, taps, filters_of, stored_ref, packed_ref)
        for copy in ahead:
            copy.wait()

    return pl.pallas_call(
        run,
        in_specs=[OUTSIDE] * 3,
        out_specs=[WHOLE] * 3,
        out_shape=layer_outputs(plan) + [filters_in_vmem(upcoming, following)],
        scratch_shapes=[
            pltpu.VMEM(maps.shape, maps.dtype),
            pltpu.SemaphoreType.DMA(()),
            padded_scratch(plan),
            filters_in_vmem(taps, kernel),
            pltpu.SemaphoreType.DMA((len(taps),)),
            pltpu.SemaphoreType.DMA((len(upcoming),)),
        ],
        compiler_params=PARAMS,
    )(in_hbm(maps), in_hbm(kernel), in_hbm(following))


def layer_of_stored(plan, stored, gathered, gain, bias, early, kernel, following, count):
    def body(padded, stored_ref, gathered_ref, gain_ref, bias_ref):
        scale, offset = join(plan, gathered_ref[...], gain_ref[...], bias_ref[...])

        def write(lanes, values):
            padded[1, inner(plan), lanes] = values

        normalize_into(plan, stored_ref, scale, offset, write)

    return conv_layer(plan, body, [in_vmem(stored), gathered, gain, bias], early, kernel, following, count)


def layer_of_moved(plan, stored, terms, maps, is_first, early, kernel, following, count):
    def body(padded, stored_ref, terms_ref, maps_ref, first_ref):
        first = jnp.broadcast_to(first_ref[...], (plan.rows, LANES)) > 0.5

        def write(lanes, values):
            arrived = padded[1, inner(plan), lanes]
            padded[1, inner(plan), lanes] = jnp.where(first, arrived, values)

        def write_line(start, rows):
            padded[1, pl.ds(plan.line + start, rows.shape[0]), :] = rows

        spread_lines(plan, maps_ref, write_line)
        terms = terms_ref[...]
        normalize_into(plan, stored_ref, terms[: plan.groups], terms[plan.groups :], write)

    operands = [in_vmem(stored), terms, in_vmem(maps), is_first]
    return conv_layer(plan, body, operands, early, kernel, following, count)


def finish(plan, stored, terms, gathered, gain, bias):
    shape = (TICKS, plan.height, plan.width, plan.images, plan.channels)

    def run(*refs):
        *refs, out_hbm, out_ref, sems = refs
        copies = []
        for tick in range(TICKS):

            def write(lanes, values, tick=tick):
                for row in range(plan.height):
                    line = values[row * plan.line : row * plan.line + plan.width * plan.images]
                    out_ref[tick, row, :, :, lanes] = line.reshape(plan.width, plan.images, LANES)

            if tick + 1 < TICKS:
                known = refs[TICKS + tick][...]
                scale, offset = known[: plan.groups], known[plan.groups :]
            else:
                scale, offset = join(plan, *(ref[...] for ref in refs[2 * TICKS - 1 :]))
            normalize_into(plan, refs[tick], scale, offset, write)
            copies.append(pltpu.make_async_copy(out_ref.at[tick], out_hbm.at[tick], sems.at[tick]))
            copies[-1].start()
        for copy in copies:
            copy.wait()

    operands = [in_vmem(value) for value in stored] + terms + [gathered, gain, bias]
    return pl.pallas_call(
        run,
        in_specs=[WHOLE] * len(operands),
        out_specs=OUTSIDE,
        out_shape=pltpu.HBM(shape, jnp.bfloat16),
        scratch_shapes=[pltpu.VMEM(shape, jnp.bfloat16), pltpu.SemaphoreType.DMA((TICKS,))],
        compiler_params=PARAMS,
    )(*operands)


def from_behind(value, axis):
    length = lax.axis_size(axis)
    return lax.ppermute(value, axis, [(i, (i + 1) % length) for i in range(length)])


def body(
    pending_section_entries,
    arriving_microsets,
    opening_filter_kernel,
    closing_filter_kernel,
    stretch_factors,
    shift_terms,
):
    _, images, height, width, channels = pending_section_entries.shape
    plan = Plan(images, height, width, channels, lax.axis_size("replica"))
    first_kernel = opening_filter_kernel[0]
    second_kernel = closing_filter_kernel[0]
    is_first = jnp.broadcast_to((lax.axis_index("section") == 0).astype(jnp.float32), (1, LANES))
    order = (1, 2, 0, 3)
    maps = jnp.transpose(pending_section_entries[0], order)
    stored, packed, early = opening_layer(plan, maps, first_kernel, second_kernel, CLOSING_AHEAD)
    kept, kept_terms = [], []
    for tick in range(TICKS):
        gathered = exchange(plan, packed)
        if tick == 0:
            gathered, gains, biases = lax.optimization_barrier((gathered, stretch_factors, shift_terms))
            gain = gains[0].reshape(2, plan.groups, LANES)
            bias = biases[0].reshape(2, plan.groups, LANES)
        last = tick + 1 == TICKS
        ahead = (None, 0) if last else (first_kernel, OPENING_AHEAD)
        stored, packed, *early = layer_of_stored(
            plan, stored, gathered, gain[0], bias[0], early, second_kernel, *ahead
        )
        kept.append(stored)
        if last:
            break
        moved = from_behind(stored, "section")
        terms = jnp.concatenate(join(plan, exchange(plan, packed), gain[1], bias[1]), axis=0)
        kept_terms.append(terms)
        terms = from_behind(terms, "section")
        arriving = jnp.transpose(arriving_microsets[tick], order)
        ahead = (second_kernel, CLOSING_AHEAD)
        stored, packed, early = layer_of_moved(
            plan, moved, terms, arriving, is_first, early[0], first_kernel, *ahead
        )
    result = finish(plan, kept, kept_terms, exchange(plan, packed), gain[1], bias[1])
    return jnp.transpose(result, (0, 3, 1, 2, 4))[None]


def solution(mesh):
    in_specs = (
        P("section", "replica", None, None, None),
        P(None, "replica", None, None, None),
        P("section", None, None, None, None),
        P("section", None, None, None, None),
        P("section", None, None),
        P("section", None, None),
    )
    out_specs = P("section", None, "replica", None, None, None)
    return jax.shard_map(body, mesh=mesh, in_specs=in_specs, out_specs=out_specs, check_vma=False)
```

```python
import jax
import jax.numpy as jnp
from jax import lax
from jax.experimental import pallas as pl
from jax.experimental.pallas import tpu as pltpu
from jax.sharding import PartitionSpec as P

TICKS = 2
LANES = 128
EPS = 1e-05


class Plan:
    def __init__(self, images, height, width, channels, members):
        self.images, self.height, self.width, self.channels = images, height, width, channels
        self.members = members
        self.wide = 16
        self.line = self.wide * images
        self.rows = height * self.line
        self.groups = channels // LANES
        self.count = images * height * width

    def real_rows(self):
        row = lax.broadcasted_iota(jnp.int32, (self.rows, LANES), 0)
        return row % self.line < self.width * self.images


def fill_shifted(plan, padded):
    line, rows, step = plan.line, plan.rows, plan.images
    padded[0, pl.ds(line, rows), :] = padded[1, pl.ds(line - step, rows), :]
    padded[2, pl.ds(line, rows), :] = padded[1, pl.ds(line + step, rows), :]


def zero_borders(plan, padded):
    border = jnp.zeros((plan.line, plan.channels), jnp.bfloat16)
    for shift in range(3):
        padded[shift, pl.ds(0, plan.line), :] = border
        padded[shift, pl.ds(plan.line + plan.rows, plan.line), :] = border


TAPS = [(0, 1), (1, 1), (2, 1), (0, 0), (1, 0), (2, 0), (0, 2), (1, 2), (2, 2)]
OPENING_AHEAD = 3.5
CLOSING_AHEAD = 4


def early_and_late(channels, count):
    early, late = [], []
    for place, (kh, kw) in enumerate(TAPS):
        split = int(channels * min(max(count - place, 0), 1))
        if split > 0:
            early.append((kh, kw, 0, split))
        if split < channels:
            late.append((kh, kw, split, channels - split))
    return early, late


def row_of(taps, place):
    return sum(size for _, _, _, size in taps[:place])


def convolve_and_measure(plan, padded, taps, filters_of, stored_ref, packed_ref):
    conv_out = None
    for tap in taps:
        kh, kw, channel, size = tap
        shifted = padded[kw, pl.ds(kh * plan.line, plan.rows), channel : channel + size]
        part = jnp.dot(shifted, filters_of(tap), preferred_element_type=jnp.float32)
        conv_out = part if conv_out is None else conv_out + part
    stored_ref[...] = conv_out.astype(jnp.bfloat16)
    real = plan.real_rows()
    means, deviations = [], []
    for group in range(plan.groups):
        values = jnp.where(real, conv_out[:, group * LANES : (group + 1) * LANES], 0.0)
        mean = jnp.sum(values, axis=0, keepdims=True) / plan.count
        centred = jnp.where(real, values - mean, 0.0)
        means.append(mean)
        deviations.append(jnp.sqrt(jnp.sum(centred * centred, axis=0, keepdims=True) / plan.count))
    packed_ref[...] = jnp.concatenate(means + deviations, axis=0)


def exchange(plan, packed):
    copies = jnp.broadcast_to(packed.astype(jnp.float16), (plan.members,) + packed.shape)
    return lax.all_to_all(copies, "replica", 0, 0).astype(jnp.float32)


def join(plan, gathered, gain, bias):
    groups = plan.groups
    means, deviations = gathered[:, :groups], gathered[:, groups:]
    mean = jnp.sum(means, axis=0) / plan.members
    apart = means - mean[None]
    var = jnp.sum(deviations * deviations + apart * apart, axis=0) / plan.members
    scale = gain * lax.rsqrt(var + EPS)
    return scale, bias - mean * scale


def normalize_into(plan, stored_ref, scale, offset, write):
    real = plan.real_rows()
    for group in range(plan.groups):
        lanes = slice(group * LANES, (group + 1) * LANES)
        values = stored_ref[:, lanes].astype(jnp.float32) * scale[group : group + 1] + offset[group : group + 1]
        write(lanes, jnp.where(real, jnp.maximum(values, 0.0), 0.0).astype(jnp.bfloat16))


def in_vmem(value):
    return pltpu.with_memory_space_constraint(value, pltpu.VMEM)


def in_hbm(value):
    return pltpu.with_memory_space_constraint(value, pltpu.HBM)


def fetch_taps(kernel_hbm, taps, target, sems):
    copies = []
    for place, (kh, kw, channel, size) in enumerate(taps):
        source = kernel_hbm.at[kh, kw, pl.ds(channel, size)]
        copies.append(pltpu.make_async_copy(source, target.at[pl.ds(row_of(taps, place), size)], sems.at[place]))
    return copies


def layer_outputs(plan):
    return [
        pltpu.VMEM((plan.rows, plan.channels), jnp.bfloat16),
        pltpu.VMEM((2 * plan.groups, LANES), jnp.float32),
    ]


def filters_in_vmem(taps, kernel):
    return pltpu.VMEM((row_of(taps, len(taps)), kernel.shape[3]), kernel.dtype)


def padded_scratch(plan):
    return pltpu.VMEM((3, plan.rows + 2 * plan.line, plan.channels), jnp.bfloat16)


WHOLE = pl.BlockSpec(memory_space=pltpu.VMEM)
OUTSIDE = pl.BlockSpec(memory_space=pltpu.HBM)
PARAMS = pltpu.CompilerParams(vmem_limit_bytes=32 << 20)


def conv_layer(plan, body, operands, early, kernel, following, count, earlier=None):
    ahead = [] if following is None else [following]
    done = [] if earlier is None else [in_vmem(earlier[0]), earlier[1]]
    shape = result_shape(plan)
    first, late = early_and_late(plan.channels, early.shape[0] / plan.channels)
    upcoming, _ = early_and_late(plan.channels, count)

    def run(*refs):
        ins, refs = refs[: len(operands)], refs[len(operands) :]
        early_ref, kernel_hbm, refs = refs[0], refs[1], refs[2:]
        next_hbm, refs = refs[: len(ahead)], refs[len(ahead) :]
        done_refs, refs = refs[: len(done)], refs[len(done) :]
        stored_ref, packed_ref, refs = refs[0], refs[1], refs[2:]
        next_early, refs = refs[: len(ahead)], refs[len(ahead) :]
        if done:
            result_hbm, *refs, result_vmem, result_sem = refs
            written = pltpu.make_async_copy(result_vmem, result_hbm.at[0], result_sem)
        padded, sides, sems, next_sems = refs
        copies = fetch_taps(kernel_hbm, late, sides, sems)
        for copy in copies:
            copy.start()
        for source, target in zip(next_hbm, next_early):
            ahead_copies = fetch_taps(source, upcoming, target, next_sems)
            for copy in ahead_copies:
                copy.start(priority=1)
            copies += ahead_copies
        zero_borders(plan, padded)
        body(padded, *ins)
        fill_shifted(plan, padded)

        def filters_of(tap):
            if tap in first:
                return early_ref[pl.ds(row_of(first, first.index(tap)), tap[3]), :]
            place = late.index(tap)
            if done and place == 0:
                terms = done_refs[1][...]
                write = map_writer(plan, result_vmem)
                normalize_into(plan, done_refs[0], terms[: plan.groups], terms[plan.groups :], write)
                written.start()
            copies[place].wait()
            return sides[pl.ds(row_of(late, place), tap[3]), :]

        convolve_and_measure(plan, padded, first + late, filters_of, stored_ref, packed_ref)
        for copy in copies[len(late) :]:
            copy.wait()
        if done:
            written.wait()

    return pl.pallas_call(
        run,
        in_specs=[WHOLE] * (len(operands) + 1) + [OUTSIDE] * (1 + len(ahead)) + [WHOLE] * len(done),
        out_specs=[WHOLE] * (2 + len(ahead)) + ([OUTSIDE] if done else []),
        out_shape=layer_outputs(plan) + [filters_in_vmem(upcoming, kernel) for kernel in ahead]
        + ([pltpu.HBM(shape, jnp.bfloat16)] if done else []),
        scratch_shapes=[
            padded_scratch(plan),
            filters_in_vmem(late, kernel),
            pltpu.SemaphoreType.DMA((len(late),)),
            pltpu.SemaphoreType.DMA((max(len(upcoming), 1),)),
        ]
        + ([pltpu.VMEM(shape[1:], jnp.bfloat16), pltpu.SemaphoreType.DMA(())] if done else []),
        compiler_params=PARAMS,
    )(*operands, in_vmem(early), in_hbm(kernel), *map(in_hbm, ahead), *done)


def result_shape(plan):
    return (TICKS, plan.height, plan.width, plan.images, plan.channels)


def map_writer(plan, out_ref):
    def write(lanes, values):
        for row in range(plan.height):
            line = values[row * plan.line : row * plan.line + plan.width * plan.images]
            out_ref[row, :, :, lanes] = line.reshape(plan.width, plan.images, LANES)

    return write


def inner(plan):
    return pl.ds(plan.line, plan.rows)


def spread_lines(plan, maps_ref, write):
    real = plan.width * plan.images
    blank = jnp.zeros((plan.line - real, plan.channels), jnp.bfloat16)
    for row in range(plan.height):
        write(row * plan.line, maps_ref[row].reshape(real, plan.channels))
        write(row * plan.line + real, blank)


def opening_layer(plan, maps, kernel, following, count):
    _, taps = early_and_late(plan.channels, 0)
    upcoming, _ = early_and_late(plan.channels, count)

    def run(maps_hbm, kernel_hbm, next_hbm, stored_ref, packed_ref, next_early, *scratch):
        maps_vmem, map_sem, padded, filters, sems, next_sems = scratch
        fetch = pltpu.make_async_copy(maps_hbm, maps_vmem, map_sem)
        fetch.start()
        copies = fetch_taps(kernel_hbm, taps, filters, sems)
        ahead = fetch_taps(next_hbm, upcoming, next_early, next_sems)
        for copy in copies[:3]:
            copy.start(priority=1)
        zero_borders(plan, padded)
        fetch.wait()
        for copy in copies[3:] + ahead:
            copy.start()

        def write(start, rows):
            padded[1, pl.ds(plan.line + start, rows.shape[0]), :] = rows

        spread_lines(plan, maps_vmem, write)
        fill_shifted(plan, padded)

        def filters_of(tap):
            place = taps.index(tap)
            copies[place].wait()
            return filters[pl.ds(row_of(taps, place), tap[3]), :]

        convolve_and_measure(plan, padded, taps, filters_of, stored_ref, packed_ref)
        for copy in ahead:
            copy.wait()

    return pl.pallas_call(
        run,
        in_specs=[OUTSIDE] * 3,
        out_specs=[WHOLE] * 3,
        out_shape=layer_outputs(plan) + [filters_in_vmem(upcoming, following)],
        scratch_shapes=[
            pltpu.VMEM(maps.shape, maps.dtype),
            pltpu.SemaphoreType.DMA(()),
            padded_scratch(plan),
            filters_in_vmem(taps, kernel),
            pltpu.SemaphoreType.DMA((len(taps),)),
            pltpu.SemaphoreType.DMA((len(upcoming),)),
        ],
        compiler_params=PARAMS,
    )(in_hbm(maps), in_hbm(kernel), in_hbm(following))


def layer_of_stored(plan, stored, gathered, gain, bias, early, kernel, following, count, earlier=None):
    def body(padded, stored_ref, gathered_ref, gain_ref, bias_ref):
        scale, offset = join(plan, gathered_ref[...], gain_ref[...], bias_ref[...])

        def write(lanes, values):
            padded[1, inner(plan), lanes] = values

        normalize_into(plan, stored_ref, scale, offset, write)

    return conv_layer(plan, body, [in_vmem(stored), gathered, gain, bias], early, kernel, following, count, earlier)


def layer_of_moved(plan, stored, terms, maps, is_first, early, kernel, following, count):
    def body(padded, stored_ref, terms_ref, maps_ref, first_ref):
        first = jnp.broadcast_to(first_ref[...], (plan.rows, LANES)) > 0.5

        def write(lanes, values):
            arrived = padded[1, inner(plan), lanes]
            padded[1, inner(plan), lanes] = jnp.where(first, arrived, values)

        def write_line(start, rows):
            padded[1, pl.ds(plan.line + start, rows.shape[0]), :] = rows

        spread_lines(plan, maps_ref, write_line)
        terms = terms_ref[...]
        normalize_into(plan, stored_ref, terms[: plan.groups], terms[plan.groups :], write)

    operands = [in_vmem(stored), terms, in_vmem(maps), is_first]
    return conv_layer(plan, body, operands, early, kernel, following, count)


def finish(plan, stored, gathered, gain, bias, result):
    def run(stored_ref, gathered_ref, gain_ref, bias_ref, _, out_hbm, out_vmem, sem):
        scale, offset = join(plan, gathered_ref[...], gain_ref[...], bias_ref[...])
        normalize_into(plan, stored_ref, scale, offset, map_writer(plan, out_vmem))
        copy = pltpu.make_async_copy(out_vmem, out_hbm.at[TICKS - 1], sem)
        copy.start()
        copy.wait()

    return pl.pallas_call(
        run,
        in_specs=[WHOLE] * 4 + [OUTSIDE],
        out_specs=OUTSIDE,
        out_shape=pltpu.HBM(result.shape, result.dtype),
        input_output_aliases={4: 0},
        scratch_shapes=[pltpu.VMEM(result.shape[1:], result.dtype), pltpu.SemaphoreType.DMA(())],
        compiler_params=PARAMS,
    )(in_vmem(stored), gathered, gain, bias, result)


def from_behind(value, axis):
    length = lax.axis_size(axis)
    return lax.ppermute(value, axis, [(i, (i + 1) % length) for i in range(length)])


def body(
    pending_section_entries,
    arriving_microsets,
    opening_filter_kernel,
    closing_filter_kernel,
    stretch_factors,
    shift_terms,
):
    _, images, height, width, channels = pending_section_entries.shape
    plan = Plan(images, height, width, channels, lax.axis_size("replica"))
    first_kernel = opening_filter_kernel[0]
    second_kernel = closing_filter_kernel[0]
    is_first = jnp.broadcast_to((lax.axis_index("section") == 0).astype(jnp.float32), (1, LANES))
    order = (1, 2, 0, 3)
    maps = jnp.transpose(pending_section_entries[0], order)
    stored, packed, early = opening_layer(plan, maps, first_kernel, second_kernel, CLOSING_AHEAD)
    earlier = None
    for tick in range(TICKS):
        gathered = exchange(plan, packed)
        if tick == 0:
            gathered, gains, biases = lax.optimization_barrier((gathered, stretch_factors, shift_terms))
            gain = gains[0].reshape(2, plan.groups, LANES)
            bias = biases[0].reshape(2, plan.groups, LANES)
        last = tick + 1 == TICKS
        ahead = (None, 0) if last else (first_kernel, OPENING_AHEAD)
        stored, packed, *rest = layer_of_stored(
            plan, stored, gathered, gain[0], bias[0], early, second_kernel, *ahead, earlier
        )
        if last:
            break
        moved = from_behind(stored, "section")
        terms = jnp.concatenate(join(plan, exchange(plan, packed), gain[1], bias[1]), axis=0)
        earlier = (stored, terms)
        terms = from_behind(terms, "section")
        arriving = jnp.transpose(arriving_microsets[tick], order)
        ahead = (second_kernel, CLOSING_AHEAD)
        stored, packed, early = layer_of_moved(
            plan, moved, terms, arriving, is_first, rest[0], first_kernel, *ahead
        )
    result = finish(plan, stored, exchange(plan, packed), gain[1], bias[1], rest[0])
    return jnp.transpose(result, (0, 3, 1, 2, 4))[None]


def solution(mesh):
    in_specs = (
        P("section", "replica", None, None, None),
        P(None, "replica", None, None, None),
        P("section", None, None, None, None),
        P("section", None, None, None, None),
        P("section", None, None),
        P("section", None, None),
    )
    out_specs = P("section", None, "replica", None, None, None)
    return jax.shard_map(body, mesh=mesh, in_specs=in_specs, out_specs=out_specs, check_vma=False)
```

```python
import jax
import jax.numpy as jnp
from jax import lax
from jax.experimental import pallas as pl
from jax.experimental.pallas import tpu as pltpu
from jax.sharding import PartitionSpec as P

TICKS = 2
LANES = 128
EPS = 1e-05


class Plan:
    def __init__(self, images, height, width, channels, members):
        self.images, self.height, self.width, self.channels = images, height, width, channels
        self.members = members
        self.wide = 16
        self.line = self.wide * images
        self.rows = height * self.line
        self.groups = channels // LANES
        self.count = images * height * width

    def real_rows(self):
        row = lax.broadcasted_iota(jnp.int32, (self.rows, LANES), 0)
        return row % self.line < self.width * self.images


def fill_shifted(plan, padded):
    line, rows, step = plan.line, plan.rows, plan.images
    padded[0, pl.ds(line, rows), :] = padded[1, pl.ds(line - step, rows), :]
    padded[2, pl.ds(line, rows), :] = padded[1, pl.ds(line + step, rows), :]


def zero_borders(plan, padded):
    border = jnp.zeros((plan.line, plan.channels), jnp.bfloat16)
    for shift in range(3):
        padded[shift, pl.ds(0, plan.line), :] = border
        padded[shift, pl.ds(plan.line + plan.rows, plan.line), :] = border


TAPS = [(0, 1), (1, 1), (2, 1), (0, 0), (1, 0), (2, 0), (0, 2), (1, 2), (2, 2)]
OPENING_AHEAD = 3.5
CLOSING_AHEAD = 4
FIRST_AHEAD = 5


def early_and_late(channels, count):
    early, late = [], []
    for place, (kh, kw) in enumerate(TAPS):
        split = int(channels * min(max(count - place, 0), 1))
        if split > 0:
            early.append((kh, kw, 0, split))
        if split < channels:
            late.append((kh, kw, split, channels - split))
    return early, late


def row_of(taps, place):
    return sum(size for _, _, _, size in taps[:place])


def convolve_and_measure(plan, padded, taps, filters_of, stored_ref, packed_ref):
    conv_out = None
    for tap in taps:
        kh, kw, channel, size = tap
        shifted = padded[kw, pl.ds(kh * plan.line, plan.rows), channel : channel + size]
        part = jnp.dot(shifted, filters_of(tap), preferred_element_type=jnp.float32)
        conv_out = part if conv_out is None else conv_out + part
    stored_ref[...] = conv_out.astype(jnp.bfloat16)
    real = plan.real_rows()
    means, deviations = [], []
    for group in range(plan.groups):
        values = jnp.where(real, conv_out[:, group * LANES : (group + 1) * LANES], 0.0)
        mean = jnp.sum(values, axis=0, keepdims=True) / plan.count
        centred = jnp.where(real, values - mean, 0.0)
        means.append(mean)
        deviations.append(jnp.sqrt(jnp.sum(centred * centred, axis=0, keepdims=True) / plan.count))
    packed_ref[...] = jnp.concatenate(means + deviations, axis=0)


def exchange(plan, packed):
    copies = jnp.broadcast_to(packed.astype(jnp.float16), (plan.members,) + packed.shape)
    return lax.all_to_all(copies, "replica", 0, 0).astype(jnp.float32)


def join(plan, gathered, gain, bias):
    groups = plan.groups
    means, deviations = gathered[:, :groups], gathered[:, groups:]
    mean = jnp.sum(means, axis=0) / plan.members
    apart = means - mean[None]
    var = jnp.sum(deviations * deviations + apart * apart, axis=0) / plan.members
    scale = gain * lax.rsqrt(var + EPS)
    return scale, bias - mean * scale


def normalize_into(plan, stored_ref, scale, offset, write):
    real = plan.real_rows()
    for group in range(plan.groups):
        lanes = slice(group * LANES, (group + 1) * LANES)
        values = stored_ref[:, lanes].astype(jnp.float32) * scale[group : group + 1] + offset[group : group + 1]
        write(lanes, jnp.where(real, jnp.maximum(values, 0.0), 0.0).astype(jnp.bfloat16))


def in_vmem(value):
    return pltpu.with_memory_space_constraint(value, pltpu.VMEM)


def in_hbm(value):
    return pltpu.with_memory_space_constraint(value, pltpu.HBM)


def fetch_taps(kernel_hbm, taps, target, sems):
    copies = []
    for place, (kh, kw, channel, size) in enumerate(taps):
        source = kernel_hbm.at[kh, kw, pl.ds(channel, size)]
        copies.append(pltpu.make_async_copy(source, target.at[pl.ds(row_of(taps, place), size)], sems.at[place]))
    return copies


def layer_outputs(plan):
    return [
        pltpu.VMEM((plan.rows, plan.channels), jnp.bfloat16),
        pltpu.VMEM((2 * plan.groups, LANES), jnp.float32),
    ]


def filters_in_vmem(taps, kernel):
    return pltpu.VMEM((row_of(taps, len(taps)), kernel.shape[3]), kernel.dtype)


def padded_scratch(plan):
    return pltpu.VMEM((3, plan.rows + 2 * plan.line, plan.channels), jnp.bfloat16)


WHOLE = pl.BlockSpec(memory_space=pltpu.VMEM)
OUTSIDE = pl.BlockSpec(memory_space=pltpu.HBM)
PARAMS = pltpu.CompilerParams(vmem_limit_bytes=32 << 20)


def conv_layer(plan, body, operands, early, kernel, following, count, earlier=None):
    ahead = [] if following is None else [following]
    done = [] if earlier is None else [in_vmem(earlier[0]), earlier[1]]
    shape = result_shape(plan)
    first, late = early_and_late(plan.channels, early.shape[0] / plan.channels)
    upcoming, _ = early_and_late(plan.channels, count)

    def run(*refs):
        ins, refs = refs[: len(operands)], refs[len(operands) :]
        early_ref, kernel_hbm, refs = refs[0], refs[1], refs[2:]
        next_hbm, refs = refs[: len(ahead)], refs[len(ahead) :]
        done_refs, refs = refs[: len(done)], refs[len(done) :]
        stored_ref, packed_ref, refs = refs[0], refs[1], refs[2:]
        next_early, refs = refs[: len(ahead)], refs[len(ahead) :]
        if done:
            result_hbm, *refs, result_vmem, result_sem = refs
            written = pltpu.make_async_copy(result_vmem, result_hbm.at[0], result_sem)
        padded, sides, sems, next_sems = refs
        copies = fetch_taps(kernel_hbm, late, sides, sems)
        for copy in copies:
            copy.start()
        for source, target in zip(next_hbm, next_early):
            ahead_copies = fetch_taps(source, upcoming, target, next_sems)
            for copy in ahead_copies:
                copy.start(priority=1)
            copies += ahead_copies
        zero_borders(plan, padded)
        body(padded, *ins)
        fill_shifted(plan, padded)

        def filters_of(tap):
            if tap in first:
                return early_ref[pl.ds(row_of(first, first.index(tap)), tap[3]), :]
            place = late.index(tap)
            if done and place == 0:
                terms = done_refs[1][...]
                write = map_writer(plan, result_vmem)
                normalize_into(plan, done_refs[0], terms[: plan.groups], terms[plan.groups :], write)
                written.start()
            copies[place].wait()
            return sides[pl.ds(row_of(late, place), tap[3]), :]

        convolve_and_measure(plan, padded, first + late, filters_of, stored_ref, packed_ref)
        for copy in copies[len(late) :]:
            copy.wait()
        if done:
            written.wait()

    return pl.pallas_call(
        run,
        in_specs=[WHOLE] * (len(operands) + 1) + [OUTSIDE] * (1 + len(ahead)) + [WHOLE] * len(done),
        out_specs=[WHOLE] * (2 + len(ahead)) + ([OUTSIDE] if done else []),
        out_shape=layer_outputs(plan) + [filters_in_vmem(upcoming, kernel) for kernel in ahead]
        + ([pltpu.HBM(shape, jnp.bfloat16)] if done else []),
        scratch_shapes=[
            padded_scratch(plan),
            filters_in_vmem(late, kernel),
            pltpu.SemaphoreType.DMA((len(late),)),
            pltpu.SemaphoreType.DMA((max(len(upcoming), 1),)),
        ]
        + ([pltpu.VMEM(shape[1:], jnp.bfloat16), pltpu.SemaphoreType.DMA(())] if done else []),
        compiler_params=PARAMS,
    )(*operands, in_vmem(early), in_hbm(kernel), *map(in_hbm, ahead), *done)


def joined(plan, gathered, gain, bias):
    def run(gathered_ref, gain_ref, bias_ref, terms_ref):
        scale, offset = join(plan, gathered_ref[...], gain_ref[...], bias_ref[...])
        terms_ref[...] = jnp.concatenate([scale, offset], axis=0)

    return pl.pallas_call(
        run,
        in_specs=[WHOLE] * 3,
        out_specs=WHOLE,
        out_shape=pltpu.VMEM((2 * plan.groups, LANES), jnp.float32),
        compiler_params=PARAMS,
    )(gathered, gain, bias)


def result_shape(plan):
    return (TICKS, plan.height, plan.width, plan.images, plan.channels)


def map_writer(plan, out_ref):
    def write(lanes, values):
        for row in range(plan.height):
            line = values[row * plan.line : row * plan.line + plan.width * plan.images]
            out_ref[row, :, :, lanes] = line.reshape(plan.width, plan.images, LANES)

    return write


def inner(plan):
    return pl.ds(plan.line, plan.rows)


def spread_lines(plan, maps_ref, write):
    real = plan.width * plan.images
    blank = jnp.zeros((plan.line - real, plan.channels), jnp.bfloat16)
    for row in range(plan.height):
        write(row * plan.line, maps_ref[row].reshape(real, plan.channels))
        write(row * plan.line + real, blank)


def opening_layer(plan, maps, kernel, following, count):
    _, taps = early_and_late(plan.channels, 0)
    upcoming, _ = early_and_late(plan.channels, count)

    def run(maps_hbm, kernel_hbm, next_hbm, stored_ref, packed_ref, next_early, *scratch):
        maps_vmem, map_sem, padded, filters, sems, next_sems = scratch
        fetch = pltpu.make_async_copy(maps_hbm, maps_vmem, map_sem)
        fetch.start()
        copies = fetch_taps(kernel_hbm, taps, filters, sems)
        ahead = fetch_taps(next_hbm, upcoming, next_early, next_sems)
        for copy in copies[:3]:
            copy.start(priority=1)
        zero_borders(plan, padded)
        fetch.wait()
        for copy in copies[3:] + ahead:
            copy.start()

        def write(start, rows):
            padded[1, pl.ds(plan.line + start, rows.shape[0]), :] = rows

        spread_lines(plan, maps_vmem, write)
        fill_shifted(plan, padded)

        def filters_of(tap):
            place = taps.index(tap)
            copies[place].wait()
            return filters[pl.ds(row_of(taps, place), tap[3]), :]

        convolve_and_measure(plan, padded, taps, filters_of, stored_ref, packed_ref)
        for copy in ahead:
            copy.wait()

    return pl.pallas_call(
        run,
        in_specs=[OUTSIDE] * 3,
        out_specs=[WHOLE] * 3,
        out_shape=layer_outputs(plan) + [filters_in_vmem(upcoming, following)],
        scratch_shapes=[
            pltpu.VMEM(maps.shape, maps.dtype),
            pltpu.SemaphoreType.DMA(()),
            padded_scratch(plan),
            filters_in_vmem(taps, kernel),
            pltpu.SemaphoreType.DMA((len(taps),)),
            pltpu.SemaphoreType.DMA((len(upcoming),)),
        ],
        compiler_params=PARAMS,
    )(in_hbm(maps), in_hbm(kernel), in_hbm(following))


def layer_of_stored(plan, stored, gathered, gain, bias, early, kernel, following, count, earlier=None):
    def body(padded, stored_ref, gathered_ref, gain_ref, bias_ref):
        scale, offset = join(plan, gathered_ref[...], gain_ref[...], bias_ref[...])

        def write(lanes, values):
            padded[1, inner(plan), lanes] = values

        normalize_into(plan, stored_ref, scale, offset, write)

    return conv_layer(plan, body, [in_vmem(stored), gathered, gain, bias], early, kernel, following, count, earlier)


def layer_of_moved(plan, stored, terms, maps, is_first, early, kernel, following, count):
    def body(padded, stored_ref, terms_ref, maps_ref, first_ref):
        first = jnp.broadcast_to(first_ref[...], (plan.rows, LANES)) > 0.5

        def write(lanes, values):
            arrived = padded[1, inner(plan), lanes]
            padded[1, inner(plan), lanes] = jnp.where(first, arrived, values)

        def write_line(start, rows):
            padded[1, pl.ds(plan.line + start, rows.shape[0]), :] = rows

        spread_lines(plan, maps_ref, write_line)
        terms = terms_ref[...]
        normalize_into(plan, stored_ref, terms[: plan.groups], terms[plan.groups :], write)

    operands = [in_vmem(stored), terms, in_vmem(maps), is_first]
    return conv_layer(plan, body, operands, early, kernel, following, count)


def finish(plan, stored, gathered, gain, bias, result):
    def run(stored_ref, gathered_ref, gain_ref, bias_ref, _, out_hbm, out_vmem, sem):
        scale, offset = join(plan, gathered_ref[...], gain_ref[...], bias_ref[...])
        normalize_into(plan, stored_ref, scale, offset, map_writer(plan, out_vmem))
        copy = pltpu.make_async_copy(out_vmem, out_hbm.at[TICKS - 1], sem)
        copy.start()
        copy.wait()

    return pl.pallas_call(
        run,
        in_specs=[WHOLE] * 4 + [OUTSIDE],
        out_specs=OUTSIDE,
        out_shape=pltpu.HBM(result.shape, result.dtype),
        input_output_aliases={4: 0},
        scratch_shapes=[pltpu.VMEM(result.shape[1:], result.dtype), pltpu.SemaphoreType.DMA(())],
        compiler_params=PARAMS,
    )(in_vmem(stored), gathered, gain, bias, result)


def from_behind(value, axis):
    length = lax.axis_size(axis)
    return lax.ppermute(value, axis, [(i, (i + 1) % length) for i in range(length)])


def body(
    pending_section_entries,
    arriving_microsets,
    opening_filter_kernel,
    closing_filter_kernel,
    stretch_factors,
    shift_terms,
):
    _, images, height, width, channels = pending_section_entries.shape
    plan = Plan(images, height, width, channels, lax.axis_size("replica"))
    first_kernel = opening_filter_kernel[0]
    second_kernel = closing_filter_kernel[0]
    is_first = jnp.broadcast_to((lax.axis_index("section") == 0).astype(jnp.float32), (1, LANES))
    order = (1, 2, 0, 3)
    maps = jnp.transpose(pending_section_entries[0], order)
    stored, packed, early = opening_layer(plan, maps, first_kernel, second_kernel, FIRST_AHEAD)
    earlier = None
    for tick in range(TICKS):
        gathered = exchange(plan, packed)
        if tick == 0:
            gathered, gains, biases = lax.optimization_barrier((gathered, stretch_factors, shift_terms))
            gain = gains[0].reshape(2, plan.groups, LANES)
            bias = biases[0].reshape(2, plan.groups, LANES)
        last = tick + 1 == TICKS
        ahead = (None, 0) if last else (first_kernel, OPENING_AHEAD)
        stored, packed, *rest = layer_of_stored(
            plan, stored, gathered, gain[0], bias[0], early, second_kernel, *ahead, earlier
        )
        if last:
            break
        moved = from_behind(stored, "section")
        terms = joined(plan, exchange(plan, packed), gain[1], bias[1])
        earlier = (stored, terms)
        terms = from_behind(terms, "section")
        arriving = jnp.transpose(arriving_microsets[tick], order)
        ahead = (second_kernel, CLOSING_AHEAD)
        stored, packed, early = layer_of_moved(
            plan, moved, terms, arriving, is_first, rest[0], first_kernel, *ahead
        )
    result = finish(plan, stored, exchange(plan, packed), gain[1], bias[1], rest[0])
    return jnp.transpose(result, (0, 3, 1, 2, 4))[None]


def solution(mesh):
    in_specs = (
        P("section", "replica", None, None, None),
        P(None, "replica", None, None, None),
        P("section", None, None, None, None),
        P("section", None, None, None, None),
        P("section", None, None),
        P("section", None, None),
    )
    out_specs = P("section", None, "replica", None, None, None)
    return jax.shard_map(body, mesh=mesh, in_specs=in_specs, out_specs=out_specs, check_vma=False)
```
